32 devices in a mesh: tile: 8 (over z, y), grp: 4 (over x, core).
Axes of the slice: x: 2, y: 2, z: 4, core: 2. Of those that a mesh axis runs over, the one named last changes fastest.
Arguments:
- kelvin_profile: float32 [90, 8, 256], P(None, 'tile'), may hold values from 0.5 to 1.5
- moisture_profile: float32 [90, 8, 256], P(None, 'tile'), may hold values from 0.1 to 3
- spreading_number: float32 [8, 256], P('tile'), may hold values from 0.05 to 0.24
- overhead_angle_measure: float32 [8, 256], P('tile'), may hold values from 0.2 to 1
- illuminated_mask: int32 [8, 256], P('tile'), may hold values 0 or 1
- radiating_tiles: int32 [2048, 1], P('tile'), may hold values from 0 to 7; in each aligned block of 256 rows (0 to 255, 256 to 511, ...) at most 64 rows name the same one
- cloudy_member_factors: float32 [224, 4096], P('grp', 'tile'), may hold values from 0.25 to 2
- arid_opacity_table: float32 [224, 90], P('grp'), may hold values from 0.003 to 0.2
- moisture_attenuation: float32 [224], P('grp'), may hold values from 0.003 to 0.05
- blackbody_share: float32 [224], P('grp'), may hold values from 0.3 to 3
- insolation_per_quadrature: float32 [224], P('grp'), may hold values from 0.3 to 3
Outputs:
- heating: float32 [90, 8, 256], P(None, 'tile')
- temp_next: float32 [90, 8, 256], P(None, 'tile')
- vapour_next: float32 [90, 8, 256], P(None, 'tile')
The draws below stay inside these ranges and needn't reach their ends.
Inputs may be any that keep to these rules, and one draw needn't show every extreme that they name: `radiating_tiles`: among the columns of one tile no owner is named more than 64 times, a bound that some block reaches.
All inputs are finite; a program needn't handle non-finite values. No bound on the sum of `illuminated_mask` on one device may be relied on, other than what follows from the above.
Results may differ from the reference program's by a relative error of at most 0.00025.
Values sent between devices are 32-bit elements; how exact they have to be, the bound alone decides.
No kernel may reach another device: no remote copies, remote signals or barrier semaphores. Data moves between devices by JAX's collectives and lax.ppermute only.
A program may use at most 64 MiB of HBM per device.

```python
import math
import jax
import jax.numpy as jnp
import numpy as np
from jax import lax

STRATA_TOTAL = 90
NG = 224
BAND_SPAN = 256
ROWS_DEV = 1
PARALLEL_BANDS = 8
CAP = 64
N_TILE = 8


def touch_ends(values, stream_key, low, top_value):
    longest = values.shape.index(max(values.shape))
    spots = []
    for shift in (0, 1):
        where = [jax.random.randint(jax.random.fold_in(stream_key, axis), (), 0, length) for axis, length in enumerate(values.shape)]
        where[longest] = (where[longest] + shift) % values.shape[longest]
        spots.append(tuple(where))
    return values.at[spots[0]].set(low).at[spots[1]].set(top_value)


def levels(key, shape, cuts, least, high):
    def one(axis_at, shards_of):
        draws = jax.random.uniform(jax.random.fold_in(jax.random.fold_in(key, 6), axis_at), (shards_of,), jnp.float32, least / len(cuts), high / len(cuts))
        return jnp.repeat(jnp.exp(draws), shape[axis_at] // shards_of).reshape((-1,) + (1,) * (len(shape) - axis_at - 1))

    gain = one(*cuts[0])
    for cut in cuts[1:]:
        gain = gain * one(*cut)
    return gain


def shared_out(stream_key, own, number, rows, count, top, limit, slope):
    ranking = jax.random.permutation(stream_key, count)
    packed, common = portions_of(count, rows * top, limit, slope, True), portions_of(count, rows * top, limit, slope, False)
    places = jnp.arange(count)

    def named(lengths, offset_by):
        used = int((lengths > 0).sum())
        fixed = max(1, used // 4)
        shifted = fixed + (places - fixed + offset_by * (used - fixed)) % max(1, count - fixed)
        return jnp.zeros((count,), jnp.int32).at[ranking[jnp.where(places < fixed, places, shifted)]].set(jnp.asarray(lengths, jnp.int32))

    lengths = jnp.where(number % 4 == 0, named(packed, number // 4), named(common, number - number // 4 - 1))
    mixed = jax.random.permutation(jax.random.fold_in(own, 3), count)
    giver, taker = mixed[0:count // 2 * 2:2], mixed[1:count // 2 * 2:2]
    margin = jnp.minimum(lengths[giver] - 1, limit - lengths[taker]) // 2
    margin = jnp.where((giver == ranking[0]) | (taker == ranking[0]) | (lengths[taker] == 0), 0, jnp.maximum(margin, 0))
    shifted = jax.random.randint(jax.random.fold_in(own, 4), (count // 2,), 0, 1 << 20) % (margin + 1)
    lengths = lengths.at[giver].add(-shifted).at[taker].add(shifted)
    items = jnp.searchsorted(jnp.cumsum(lengths), jnp.arange(rows * top), side="right").astype(jnp.int32)
    listing = items.reshape(top, rows).T
    listing = listing[jax.random.permutation(jax.random.fold_in(own, 1), rows)]
    offset_by = jax.random.randint(jax.random.fold_in(own, 2), (rows, 1), 0, top)
    return jnp.take_along_axis(listing, (jnp.arange(top)[None, :] + offset_by) % top, axis=1)


def portions_of(number_of, total, limit, skew, full):
    portions = [(1 << 20) // math.isqrt(grade ** skew) + 1 for grade in range(1, number_of + 1)]
    largest = limit if full else min(limit, max(-(-total // number_of), total * portions[0] // sum(portions)))
    least = 1 if total - largest >= number_of - 1 else 0
    counts, surplus = [largest] + [least] * (number_of - 1), total - largest - least * (number_of - 1)
    while surplus > 0:
        movable = [i for i in range(1, number_of) if counts[i] < largest] or [i for i in range(1, number_of) if counts[i] < limit]
        pool, budget = sum([portions[i] for i in movable]), surplus
        for i in movable:
            more = min(limit - counts[i], max(1, budget * portions[i] // pool), surplus)
            counts[i] = counts[i] + more
            surplus = surplus - more
    return np.array(counts)


def setup_inputs(seed: int = 0) -> dict:
    seeds = jax.random.split(jax.random.key(seed), 12)
    kelvin_profile = jnp.clip(0.5 + 1.0 * jax.random.uniform(seeds[0], (STRATA_TOTAL, PARALLEL_BANDS, BAND_SPAN), jnp.float32) ** levels(seeds[0], (STRATA_TOTAL, PARALLEL_BANDS, BAND_SPAN), ((1, 8),), -0.2, 0.2), 0.5, 1.5)
    moisture_profile = jnp.clip(0.1 + 2.9 * jax.random.uniform(seeds[1], (STRATA_TOTAL, PARALLEL_BANDS, BAND_SPAN), jnp.float32) ** levels(seeds[1], (STRATA_TOTAL, PARALLEL_BANDS, BAND_SPAN), ((1, 8),), -0.2, 0.2), 0.1, 3.0)
    spreading_number = jnp.clip(0.05 + 0.19 * jax.random.uniform(seeds[2], (PARALLEL_BANDS, BAND_SPAN), jnp.float32) ** levels(seeds[2], (PARALLEL_BANDS, BAND_SPAN), ((0, 8),), -0.2, 0.2), 0.05, 0.24)
    overhead_angle_measure = jnp.clip(0.2 + 0.8 * jax.random.uniform(seeds[3], (PARALLEL_BANDS, BAND_SPAN), jnp.float32) ** levels(seeds[3], (PARALLEL_BANDS, BAND_SPAN), ((0, 8),), -0.2, 0.2), 0.2, 1.0)
    illuminated_mask = touch_ends((jax.random.randint(seeds[4], (PARALLEL_BANDS, BAND_SPAN), 0, 2) < 1).astype(jnp.int32), jax.random.fold_in(seeds[4], 1), 0, 1)
    radiating_tiles_keys = jax.random.split(jax.random.fold_in(seeds[5], 1), (PARALLEL_BANDS * BAND_SPAN) // (ROWS_DEV * BAND_SPAN))
    radiating_tiles_turns = jax.random.permutation(jax.random.fold_in(seeds[5], 3), (PARALLEL_BANDS * BAND_SPAN) // (ROWS_DEV * BAND_SPAN))
    radiating_tiles = jax.vmap(lambda own, number: shared_out(jax.random.fold_in(seeds[5], 2), own, number, ROWS_DEV * BAND_SPAN, N_TILE, 1, CAP, 1))(radiating_tiles_keys, radiating_tiles_turns).reshape((PARALLEL_BANDS * BAND_SPAN, 1))
    cloudy_member_factors = jnp.clip(0.25 + 1.75 * jax.random.uniform(seeds[6], (NG, N_TILE * N_TILE * CAP), jnp.float32) ** levels(seeds[6], (NG, N_TILE * N_TILE * CAP), ((0, 4), (1, 8)), -0.2, 0.2), 0.25, 2.0)
    arid_opacity_table = jnp.clip(jnp.exp(math.log(0.2) - 4.199705 * jax.random.uniform(seeds[7], (NG, STRATA_TOTAL), jnp.float32) ** levels(seeds[7], (NG, STRATA_TOTAL), ((0, 4),), -0.2, 0.2)), 0.003, 0.2)
    moisture_attenuation = jnp.clip(jnp.exp(math.log(0.05) - 2.8134107 * jax.random.uniform(seeds[8], (NG,), jnp.float32) ** levels(seeds[8], (NG,), ((0, 4),), -0.2, 0.2)), 0.003, 0.05)
    blackbody_share = jnp.clip(jnp.exp(math.log(3.0) - 2.3025851 * jax.random.uniform(seeds[9], (NG,), jnp.float32) ** levels(seeds[9], (NG,), ((0, 4),), -0.2, 0.2)), 0.3, 3.0)
    insolation_per_quadrature = jnp.clip(jnp.exp(math.log(3.0) - 2.3025851 * jax.random.uniform(seeds[10], (NG,), jnp.float32) ** levels(seeds[10], (NG,), ((0, 4),), -0.2, 0.2)), 0.3, 3.0)
    return dict(kelvin_profile=kelvin_profile, moisture_profile=moisture_profile, spreading_number=spreading_number, overhead_angle_measure=overhead_angle_measure, illuminated_mask=illuminated_mask, radiating_tiles=radiating_tiles, cloudy_member_factors=cloudy_member_factors, arid_opacity_table=arid_opacity_table, moisture_attenuation=moisture_attenuation, blackbody_share=blackbody_share, insolation_per_quadrature=insolation_per_quadrature)


def diffuse(atmosphere_variables, spreading_number):
    padded = jnp.pad(atmosphere_variables, ((0, 0), (0, 0), (1, 1), (0, 0)))
    eastern = jnp.roll(atmosphere_variables, -1, axis=3)
    western = jnp.roll(atmosphere_variables, 1, axis=3)
    return atmosphere_variables + spreading_number * (padded[:, :, :-2] + padded[:, :, 2:] + eastern + western - 4.0 * atmosphere_variables)


def evaluate_warming(kelvin_profile, moisture_profile, overhead_angle_value, illuminated_marker, profile_window, arid_multiplier, moisture_multiplier, radiance_share_table, sunshine_multiplier):
    gpoints, strata_mesh = arid_multiplier.shape
    bundle = math.gcd(gpoints, 4)
    bundles = gpoints // bundle
    lower_mask = (jnp.arange(strata_mesh)[None, :] < jnp.arange(strata_mesh + 1)[:, None]).astype(jnp.float32)
    upper_mask = 1.0 - lower_mask

    def layer_pass(pieces):
        dry_part, vapour_part, radiance_share_piece, solar_part, sub_part = pieces
        thickness = dry_part[:, :, None] + (vapour_part[:, None] * sub_part)[:, None, :] * moisture_profile[None]
        column_depth = jnp.einsum("lk,gkm->glm", lower_mask, thickness, precision=lax.Precision.HIGHEST)
        growth = jnp.exp(column_depth)
        damped = jnp.exp(-column_depth)
        infrared_radiance = radiance_share_piece[:, None, None] * kelvin_profile[None]
        downward = damped * jnp.einsum("lk,gkm->glm", lower_mask, infrared_radiance * growth[:, :strata_mesh] * jnp.expm1(thickness), precision=lax.Precision.HIGHEST)
        floor_term = infrared_radiance[:, strata_mesh - 1] * damped[:, strata_mesh]
        upward = growth * (floor_term[:, None, :] - jnp.einsum("lk,gkm->glm", upper_mask, infrared_radiance * damped[:, :strata_mesh] * jnp.expm1(-thickness), precision=lax.Precision.HIGHEST))
        sunbeam = solar_part[:, None, None] * illuminated_marker[None, None, :] * jnp.exp(-column_depth / overhead_angle_value[None, None, :])
        fluxes = downward - upward + sunbeam
        return jnp.sum(fluxes[:, :strata_mesh] - fluxes[:, 1:], axis=0)

    spectral = lax.map(layer_pass, (arid_multiplier.reshape(bundles, bundle, strata_mesh), moisture_multiplier.reshape(bundles, bundle), radiance_share_table.reshape(bundles, bundle), sunshine_multiplier.reshape(bundles, bundle), profile_window.reshape(bundles, bundle, profile_window.shape[1])))
    return jnp.sum(spectral, axis=0)


def reference(kelvin_profile, moisture_profile, spreading_number, overhead_angle_measure, illuminated_mask, radiating_tiles, cloudy_member_factors, arid_opacity_table, moisture_attenuation, blackbody_share, insolation_per_quadrature):
    atmosphere_variables = jnp.stack([kelvin_profile, moisture_profile])
    for repeat in range(2):
        atmosphere_variables = diffuse(atmosphere_variables, spreading_number)
    temp_dyn = atmosphere_variables[0]
    vapour_next = atmosphere_variables[1]
    columns = PARALLEL_BANDS * BAND_SPAN
    per_tile = ROWS_DEV * BAND_SPAN
    owner_ids = radiating_tiles[:, 0].reshape(N_TILE, per_tile)
    matches = (owner_ids[:, :, None] == jnp.arange(N_TILE, dtype=jnp.int32)[None, None, :]).astype(jnp.int32)
    position = jnp.sum((jnp.cumsum(matches, axis=1) - 1) * matches, axis=2)
    slot_index = (owner_ids * (N_TILE * CAP) + jnp.arange(N_TILE, dtype=jnp.int32)[:, None] * CAP + position).reshape(columns).astype(jnp.int32)
    picked = jnp.take(cloudy_member_factors, slot_index, axis=1)
    overhead_angle_value = overhead_angle_measure.reshape(columns)
    illuminated_marker = overhead_angle_value * illuminated_mask.reshape(columns).astype(jnp.float32)
    summed = evaluate_warming(temp_dyn.reshape(STRATA_TOTAL, columns), vapour_next.reshape(STRATA_TOTAL, columns), overhead_angle_value, illuminated_marker, picked, arid_opacity_table, moisture_attenuation, blackbody_share, insolation_per_quadrature)
    heating = (summed / NG).reshape(STRATA_TOTAL, PARALLEL_BANDS, BAND_SPAN)
    return heating, temp_dyn + heating, vapour_next
```

```python
import functools
import math

import jax
import jax.numpy as jnp
from jax import lax
from jax.experimental import pallas as pl
from jax.experimental.pallas import tpu as pltpu
from jax.sharding import PartitionSpec as P

LOG2E = math.log2(math.e)
VM = pl.BlockSpec(memory_space=pltpu.VMEM)


def kernel_call(body, out_shapes, scratch=(), flops=1 << 22, name=None):
    return pl.pallas_call(
        body,
        out_shape=[jax.ShapeDtypeStruct(s, jnp.float32) for s in out_shapes],
        out_specs=[VM] * len(out_shapes),
        scratch_shapes=list(scratch),
        compiler_params=pltpu.CompilerParams(vmem_limit_bytes=24 << 20),
        cost_estimate=pl.CostEstimate(flops=flops, bytes_accessed=1 << 21, transcendentals=0),
        name=name,
    )


def split3(x):
    high = x.astype(jnp.bfloat16)
    rest = x - high.astype(jnp.float32)
    middle = rest.astype(jnp.bfloat16)
    low = (rest - middle.astype(jnp.float32)).astype(jnp.bfloat16)
    return high, middle, low


def column_of(row):
    n = row.shape[1]
    r = lax.broadcasted_iota(jnp.int32, (n, n), 0)
    c = lax.broadcasted_iota(jnp.int32, (n, n), 1)
    return jnp.sum(jnp.where(r == c, jnp.broadcast_to(row, (n, n)), 0.0), axis=1, keepdims=True)


def around(v):
    width = v.shape[1]
    return pltpu.roll(v, width - 1, 1) + pltpu.roll(v, 1, 1) - 4.0 * v


def pack_kernel(cap, kelvin, moisture, spread, factors, fields, blocks):
    levels = kelvin.shape[0]
    tiles, rows, _ = blocks.shape
    top = factors.shape[0] - rows
    lane = lax.broadcasted_iota(jnp.int32, (rows, 2 * cap), 1)
    for pair in range(tiles // 2):
        first = factors[0:rows, pair * 2 * cap : (pair + 1) * 2 * cap]
        second = factors[top : top + rows, pair * 2 * cap : (pair + 1) * 2 * cap]
        blocks[2 * pair] = jnp.where(lane < cap, first, pltpu.roll(second, cap, 1))
        blocks[2 * pair + 1] = jnp.where(lane < cap, pltpu.roll(first, cap, 1), second)
    stack_fields(levels, kelvin, moisture, spread, fields)


def stack_fields(levels, kelvin, moisture, spread, fields):
    for l in range(levels):
        fields[l : l + 1, :] = kelvin[l]
        fields[levels + l : levels + l + 1, :] = moisture[l]
    fields[2 * levels : 2 * levels + 1, :] = spread[...]
    rest = fields.shape[0] - 2 * levels - 1
    if rest:
        fields[2 * levels + 1 :, :] = jnp.zeros((rest, fields.shape[1]), jnp.float32)


def fields_kernel(kelvin, moisture, spread, fields):
    stack_fields(kelvin.shape[0], kelvin, moisture, spread, fields)


def gather_kernel(cap, tiles, packed, levels, homed, owners, vapour, arid, fields, weights, dry, base):
    columns = owners.shape[1]
    gpoints = arid.shape[0]
    owner = owners[...]
    matches = lax.broadcasted_iota(jnp.int32, (tiles, columns), 0) == owner
    member = matches.astype(jnp.float32)
    r = lax.broadcasted_iota(jnp.int32, (columns, columns), 0)
    c = lax.broadcasted_iota(jnp.int32, (columns, columns), 1)
    earlier = (r < c).astype(jnp.float32).astype(jnp.bfloat16)
    counts = jnp.dot(member.astype(jnp.bfloat16), earlier, preferred_element_type=jnp.float32)
    rank = jnp.sum(jnp.where(matches, counts, 0.0), axis=0, keepdims=True)
    slot = owner * cap + rank.astype(jnp.int32)
    choice = (lax.broadcasted_iota(jnp.int32, (tiles * cap, columns), 0) == slot).astype(jnp.float32)
    choice = choice.astype(jnp.bfloat16)
    if packed:
        rows = homed.shape[1]
        lane = lax.broadcasted_iota(jnp.int32, (rows, 2 * cap), 1)
        lower, upper = [], []
        for pair in range(tiles // 2):
            first, second = homed[2 * pair], homed[2 * pair + 1]
            lower.append(jnp.where(lane < cap, first, pltpu.roll(second, cap, 1)))
            upper.append(jnp.where(lane < cap, pltpu.roll(first, cap, 1), second))
        lower = jnp.concatenate(lower, axis=1)
        upper = jnp.concatenate(upper, axis=1)[2 * rows - gpoints :]
        table = jnp.concatenate([lower, upper], axis=0)
    else:
        table = homed[...]
    picked = 0.0
    for part in split3(table):
        picked = picked + jnp.dot(part, choice, preferred_element_type=jnp.float32)
    weights[...] = picked * (column_of(vapour[...]) * -LOG2E)
    for l in range(levels):
        dry[l] = jnp.broadcast_to(arid[:, l : l + 1] * -LOG2E, (gpoints, dry.shape[2]))
    f = fields[...]
    spread = fields[2 * levels : 2 * levels + 1, :]
    f = f + spread * around(f)
    base[...] = f + spread * around(f)


def side_kernel(levels, fields, near, far, base, share, total):
    spread = fields[2 * levels : 2 * levels + 1, :]
    near_spread = near[2 * levels : 2 * levels + 1, :]
    f = near[...]
    near_next = f + near_spread * (far[...] + fields[...] + around(f))
    v = spread * f
    part = v + spread * (around(v) + near_next)
    share[...] = part
    total[...] = base[...] + part


def radiation_kernel(
    levels, gpoints, base, share, weights, dry, angle, lit, black, solar, part, vapour, temp, rest, sums
):
    width = base.shape[1]
    blocks = gpoints // 8
    f = base[...] + share[...]
    for l in range(levels):
        temp[l] = f[l : l + 1]
        vapour[l] = f[levels + l : levels + l + 1]
    black_column = jnp.broadcast_to(column_of(black[...]), (gpoints, 128))
    solar_column = jnp.broadcast_to(column_of(solar[...]), (gpoints, 128))
    unroll = max(u for u in range(1, 11) if levels % u == 0)
    for half in range(width // 128):
        at = slice(half * 128, (half + 1) * 128)
        mu = jnp.broadcast_to(angle[:, at], (8, 128))
        inverse = 1.0 / mu
        marker = mu * jnp.broadcast_to(lit[:, at].astype(jnp.float32), (8, 128))
        share_of = [black_column[8 * b : 8 * b + 8] for b in range(blocks)]
        weight = [weights[8 * b : 8 * b + 8, at] for b in range(blocks)]
        beams = tuple(solar_column[8 * b : 8 * b + 8] * marker for b in range(blocks))
        zero = tuple(jnp.zeros((8, 128), jnp.float32) for b in range(blocks))

        def down_level(l, carry):
            down, beam = carry
            warm = jnp.broadcast_to(temp[l, :, at], (8, 128))
            wet = jnp.broadcast_to(vapour[l, :, at], (8, 128))
            new_down, new_beam, acc = [], [], None
            for b in range(blocks):
                tau = dry[l, 8 * b : 8 * b + 8, :] + weight[b] * wet
                lost = 1.0 - jnp.exp2(tau)
                rest[l, 8 * b : 8 * b + 8, at] = lost
                step = lost * (down[b] - share_of[b] * warm)
                after = beam[b] * jnp.exp2(tau * inverse)
                net = step + (beam[b] - after)
                acc = net if acc is None else acc + net
                new_down.append(down[b] - step)
                new_beam.append(after)
            sums[half, pl.ds(pl.multiple_of(l * 8, 8), 8), :] = acc
            return tuple(new_down), tuple(new_beam)

        def up_level(i, up):
            l = levels - 1 - i
            warm = jnp.broadcast_to(temp[l, :, at], (8, 128))
            new_up, acc = [], None
            for b in range(blocks):
                step = rest[l, 8 * b : 8 * b + 8, at] * (share_of[b] * warm - up[b])
                acc = step if acc is None else acc + step
                new_up.append(up[b] + step)
            where = pl.ds(pl.multiple_of(l * 8, 8), 8)
            sums[half, where, :] = sums[half, where, :] - acc
            return tuple(new_up)

        lax.fori_loop(0, levels, down_level, (zero, beams), unroll=unroll)
        floor = jnp.broadcast_to(temp[levels - 1, :, at], (8, 128))
        lax.fori_loop(0, levels, up_level, tuple(s * floor for s in share_of), unroll=unroll)
    for half in range(width // 128):
        at = slice(half * 128, (half + 1) * 128)
        total = sums[half, pl.ds(0, levels, stride=8), :]
        for s in range(1, 8):
            total = total + sums[half, pl.ds(s, levels, stride=8), :]
        part[:, at] = total


def final_kernel(scale, one, two, temp, heating, temp_next):
    levels = one.shape[0]
    heat = (one[...] + two[...]) * scale
    for l in range(levels):
        heating[l] = heat[l : l + 1]
        temp_next[l] = temp[l] + heat[l : l + 1]


def on_device(
    n_tile,
    n_grp,
    kelvin,
    moisture,
    spreading_number,
    angle,
    lit,
    owners,
    factors,
    arid,
    vapour_absorption,
    black,
    solar,
):
    levels, rows, width = kelvin.shape
    gpoints, slots = factors.shape
    cap = slots // n_tile
    total_g = gpoints * n_grp
    if rows != 1 or n_grp & (n_grp - 1) or n_grp < 2 or gpoints % 8 or width % 128:
        raise ValueError("unsupported shapes")
    stacked = -(-(2 * levels + 1) // 8) * 8
    packed = 2 * cap == 128 and gpoints % 16 == 8 and n_tile % 2 == 0
    if packed:
        half = (gpoints + 8) // 2
        fields, blocks = kernel_call(
            functools.partial(pack_kernel, cap), [(stacked, width), (n_tile, half, 128)], name="pack"
        )(kelvin, moisture, spreading_number, factors)
        homed = lax.all_to_all(blocks, "tile", split_axis=0, concat_axis=0, tiled=True)
    else:
        (fields,) = kernel_call(fields_kernel, [(stacked, width)], name="pack")(
            kelvin, moisture, spreading_number
        )
        blocks = factors.reshape(gpoints, n_tile, cap)
        homed = lax.all_to_all(blocks, "tile", split_axis=1, concat_axis=1, tiled=True)
        homed = homed.reshape(gpoints, slots)

    def from_side(distance):
        pairs = []
        for t in range(n_tile):
            for g in range(n_grp):
                s = t - distance if g % 2 == 0 else t + distance
                if 0 <= s < n_tile:
                    pairs.append((s * n_grp + g, t * n_grp + g))
        return lax.ppermute(fields, ("tile", "grp"), pairs)

    def swapped(x, bit):
        return lax.ppermute(x, "grp", [(i, i ^ bit) for i in range(n_grp)])

    near = from_side(1)
    far = from_side(2)
    weights, dry, base = kernel_call(
        functools.partial(gather_kernel, cap, n_tile, packed, levels),
        [(gpoints, width), (levels, gpoints, 128), (stacked, width)],
        name="gather",
    )(homed, owners.reshape(1, width), vapour_absorption.reshape(1, gpoints), arid, fields)
    share, mine = kernel_call(
        functools.partial(side_kernel, levels), [(stacked, width)] * 2, name="side"
    )(fields, near, far, base)
    other = swapped(share, 1)
    part, vapour_next, temp = kernel_call(
        functools.partial(radiation_kernel, levels, gpoints),
        [(levels, width), (levels, 1, width), (levels, 1, width)],
        scratch=[
            pltpu.VMEM((levels, gpoints, width), jnp.float32),
            pltpu.VMEM((width // 128, levels * 8, 128), jnp.float32),
        ],
        name="radiation",
    )(mine, other, weights, dry, angle, lit, black.reshape(1, gpoints), solar.reshape(1, gpoints))
    bit = 1
    while 2 * bit < n_grp:
        part = part + swapped(part, bit)
        bit *= 2
    heating, temp_next = kernel_call(
        functools.partial(final_kernel, 1.0 / total_g), [(levels, 1, width)] * 2, name="final"
    )(part, swapped(part, bit), temp)
    return heating, temp_next, vapour_next


def solution(mesh):
    in_specs = (
        P(None, "tile", None),
        P(None, "tile", None),
        P("tile", None),
        P("tile", None),
        P("tile", None),
        P("tile", None),
        P("grp", "tile"),
        P("grp", None),
        P("grp"),
        P("grp"),
        P("grp"),
    )
    out_specs = (P(None, "tile", None), P(None, "tile", None), P(None, "tile", None))
    body = functools.partial(on_device, mesh.shape["tile"], mesh.shape["grp"])
    return jax.shard_map(body, mesh=mesh, in_specs=in_specs, out_specs=out_specs, check_vma=False)
```

```python
import functools
import math

import jax
import jax.numpy as jnp
from jax import lax
from jax.experimental import pallas as pl
from jax.experimental.pallas import tpu as pltpu
from jax.sharding import PartitionSpec as P

LOG2E = math.log2(math.e)
VM = pl.BlockSpec(memory_space=pltpu.VMEM)
FAR = pl.BlockSpec(memory_space=pltpu.HBM)


def kernel_call(body, outs, scratch=(), in_specs=None, flops=1 << 22, name=None):
    return pl.pallas_call(
        body,
        out_shape=[o if hasattr(o, "dtype") else jax.ShapeDtypeStruct(o, jnp.float32) for o in outs],
        out_specs=[VM] * len(outs),
        scratch_shapes=list(scratch),
        compiler_params=pltpu.CompilerParams(vmem_limit_bytes=24 << 20),
        cost_estimate=pl.CostEstimate(flops=flops, bytes_accessed=1 << 21, transcendentals=0),
        name=name,
        **({} if in_specs is None else {"in_specs": in_specs}),
    )


def split3(x):
    high = x.astype(jnp.bfloat16)
    rest = x - high.astype(jnp.float32)
    middle = rest.astype(jnp.bfloat16)
    low = (rest - middle.astype(jnp.float32)).astype(jnp.bfloat16)
    return high, middle, low


def column_of(row):
    n = row.shape[1]
    r = lax.broadcasted_iota(jnp.int32, (n, n), 0)
    c = lax.broadcasted_iota(jnp.int32, (n, n), 1)
    return jnp.sum(jnp.where(r == c, jnp.broadcast_to(row, (n, n)), 0.0), axis=1, keepdims=True)


def around(v):
    width = v.shape[1]
    return pltpu.roll(v, width - 1, 1) + pltpu.roll(v, 1, 1) - 4.0 * v


def pack_kernel(cap, packed, kept, *refs):
    n_in = kept + 3 + packed
    given, rest = refs[:n_in], refs[n_in:]
    outs, scratch, sems = rest[: 1 + packed + kept], rest[1 + packed + kept : -1], rest[-1]
    targets = tuple(scratch) + tuple(outs[1 + packed :])
    copies = [pltpu.make_async_copy(g, t, sems.at[i]) for i, (g, t) in enumerate(zip(given, targets))]
    for copy in copies:
        copy.start()
    fields = outs[0]
    if packed:
        factors, blocks = scratch[0], outs[1]
        tiles, rows, _ = blocks.shape
        top = factors.shape[0] - rows
        lane = lax.broadcasted_iota(jnp.int32, (rows, 2 * cap), 1)
        copies[0].wait()
        for pair in range(tiles // 2):
            first = factors[0:rows, pair * 2 * cap : (pair + 1) * 2 * cap]
            second = factors[top : top + rows, pair * 2 * cap : (pair + 1) * 2 * cap]
            blocks[2 * pair] = jnp.where(lane < cap, first, pltpu.roll(second, cap, 1))
            blocks[2 * pair + 1] = jnp.where(lane < cap, pltpu.roll(first, cap, 1), second)
    kelvin, moisture, spread = scratch[packed:]
    for copy in copies[packed : packed + 3]:
        copy.wait()
    levels = kelvin.shape[0]
    for l in range(levels):
        fields[l : l + 1, :] = kelvin[l]
        fields[levels + l : levels + l + 1, :] = moisture[l]
    fields[2 * levels : 2 * levels + 1, :] = spread[...]
    left = fields.shape[0] - 2 * levels - 1
    if left:
        fields[2 * levels + 1 :, :] = jnp.zeros((left, fields.shape[1]), jnp.float32)
    for copy in copies[packed + 3 :]:
        copy.wait()


def gather_kernel(cap, tiles, packed, levels, homed, owners, vapour, arid, fields, weights, dry, base):
    columns = owners.shape[1]
    gpoints = arid.shape[0]
    owner = owners[...]
    matches = lax.broadcasted_iota(jnp.int32, (tiles, columns), 0) == owner
    member = matches.astype(jnp.float32)
    r = lax.broadcasted_iota(jnp.int32, (columns, columns), 0)
    c = lax.broadcasted_iota(jnp.int32, (columns, columns), 1)
    earlier = (r < c).astype(jnp.float32).astype(jnp.bfloat16)
    counts = jnp.dot(member.astype(jnp.bfloat16), earlier, preferred_element_type=jnp.float32)
    rank = jnp.sum(jnp.where(matches, counts, 0.0), axis=0, keepdims=True)
    slot = owner * cap + rank.astype(jnp.int32)
    choice = (lax.broadcasted_iota(jnp.int32, (tiles * cap, columns), 0) == slot).astype(jnp.float32)
    choice = choice.astype(jnp.bfloat16)
    if packed:
        rows = homed.shape[1]
        lane = lax.broadcasted_iota(jnp.int32, (rows, 2 * cap), 1)
        lower, upper = [], []
        for pair in range(tiles // 2):
            first, second = homed[2 * pair], homed[2 * pair + 1]
            lower.append(jnp.where(lane < cap, first, pltpu.roll(second, cap, 1)))
            upper.append(jnp.where(lane < cap, pltpu.roll(first, cap, 1), second))
        lower = jnp.concatenate(lower, axis=1)
        upper = jnp.concatenate(upper, axis=1)[2 * rows - gpoints :]
        table = jnp.concatenate([lower, upper], axis=0)
    else:
        table = homed[...]
    picked = 0.0
    for part in split3(table):
        picked = picked + jnp.dot(part, choice, preferred_element_type=jnp.float32)
    weights[...] = picked * (column_of(vapour[...]) * -LOG2E)
    for l in range(levels):
        dry[l] = jnp.broadcast_to(arid[:, l : l + 1] * -LOG2E, (gpoints, dry.shape[2]))
    f = fields[...]
    spread = fields[2 * levels : 2 * levels + 1, :]
    f = f + spread * around(f)
    base[...] = f + spread * around(f)


def side_kernel(levels, fields, near, far, base, share, total):
    spread = fields[2 * levels : 2 * levels + 1, :]
    near_spread = near[2 * levels : 2 * levels + 1, :]
    f = near[...]
    near_next = f + near_spread * (far[...] + fields[...] + around(f))
    v = spread * f
    part = v + spread * (around(v) + near_next)
    share[...] = part
    total[...] = base[...] + part


def radiation_kernel(
    levels, gpoints, base, share, weights, dry, angle, lit, black, solar, part, vapour, temp, rest, sums
):
    width = base.shape[1]
    blocks = gpoints // 8
    f = base[...] + share[...]
    for l in range(levels):
        temp[l] = f[l : l + 1]
        vapour[l] = f[levels + l : levels + l + 1]
    black_column = jnp.broadcast_to(column_of(black[...]), (gpoints, 128))
    solar_column = jnp.broadcast_to(column_of(solar[...]), (gpoints, 128))
    unroll = max(u for u in range(1, 11) if levels % u == 0)
    for half in range(width // 128):
        at = slice(half * 128, (half + 1) * 128)
        mu = jnp.broadcast_to(angle[:, at], (8, 128))
        inverse = 1.0 / mu
        marker = mu * jnp.broadcast_to(lit[:, at].astype(jnp.float32), (8, 128))
        share_of = [black_column[8 * b : 8 * b + 8] for b in range(blocks)]
        weight = [weights[8 * b : 8 * b + 8, at] for b in range(blocks)]
        beams = tuple(solar_column[8 * b : 8 * b + 8] * marker for b in range(blocks))
        zero = tuple(jnp.zeros((8, 128), jnp.float32) for b in range(blocks))

        def down_level(l, carry):
            down, beam = carry
            warm = jnp.broadcast_to(temp[l, :, at], (8, 128))
            wet = jnp.broadcast_to(vapour[l, :, at], (8, 128))
            new_down, new_beam, acc = [], [], None
            for b in range(blocks):
                tau = dry[l, 8 * b : 8 * b + 8, :] + weight[b] * wet
                lost = 1.0 - jnp.exp2(tau)
                rest[l, 8 * b : 8 * b + 8, at] = lost
                step = lost * (down[b] - share_of[b] * warm)
                after = beam[b] * jnp.exp2(tau * inverse)
                net = step + (beam[b] - after)
                acc = net if acc is None else acc + net
                new_down.append(down[b] - step)
                new_beam.append(after)
            sums[half, pl.ds(pl.multiple_of(l * 8, 8), 8), :] = acc
            return tuple(new_down), tuple(new_beam)

        def up_level(i, up):
            l = levels - 1 - i
            warm = jnp.broadcast_to(temp[l, :, at], (8, 128))
            new_up, acc = [], None
            for b in range(blocks):
                step = rest[l, 8 * b : 8 * b + 8, at] * (share_of[b] * warm - up[b])
                acc = step if acc is None else acc + step
                new_up.append(up[b] + step)
            where = pl.ds(pl.multiple_of(l * 8, 8), 8)
            sums[half, where, :] = sums[half, where, :] - acc
            return tuple(new_up)

        lax.fori_loop(0, levels, down_level, (zero, beams), unroll=unroll)
        floor = jnp.broadcast_to(temp[levels - 1, :, at], (8, 128))
        lax.fori_loop(0, levels, up_level, tuple(s * floor for s in share_of), unroll=unroll)
    for half in range(width // 128):
        at = slice(half * 128, (half + 1) * 128)
        total = sums[half, pl.ds(0, levels, stride=8), :]
        for s in range(1, 8):
            total = total + sums[half, pl.ds(s, levels, stride=8), :]
        part[:, at] = total


def final_kernel(scale, one, two, temp, heating, temp_next):
    levels = one.shape[0]
    heat = (one[...] + two[...]) * scale
    for l in range(levels):
        heating[l] = heat[l : l + 1]
        temp_next[l] = temp[l] + heat[l : l + 1]


def on_device(
    n_tile,
    n_grp,
    kelvin,
    moisture,
    spreading_number,
    angle,
    lit,
    owners,
    factors,
    arid,
    vapour_absorption,
    black,
    solar,
):
    levels, rows, width = kelvin.shape
    gpoints, slots = factors.shape
    cap = slots // n_tile
    total_g = gpoints * n_grp
    if rows != 1 or n_grp & (n_grp - 1) or n_grp < 2 or gpoints % 8 or width % 128:
        raise ValueError("unsupported shapes")
    stacked = -(-(2 * levels + 1) // 8) * 8
    packed = 2 * cap == 128 and gpoints % 16 == 8 and n_tile % 2 == 0
    half = (gpoints + 8) // 2
    inputs = [factors] * packed + [kelvin, moisture, spreading_number]
    row = (1, gpoints)
    small = [owners.reshape(1, width), vapour_absorption.reshape(row), arid]
    small += [angle, lit, black.reshape(row), solar.reshape(row)]
    outs = [jax.ShapeDtypeStruct((stacked, width), jnp.float32)]
    outs += [jax.ShapeDtypeStruct((n_tile, half, 128), jnp.float32)] * packed
    results = kernel_call(
        functools.partial(pack_kernel, cap, packed, len(small)),
        outs + [jax.ShapeDtypeStruct(v.shape, v.dtype) for v in small],
        scratch=[pltpu.VMEM(v.shape, v.dtype) for v in inputs]
        + [pltpu.SemaphoreType.DMA((len(inputs) + len(small),))],
        in_specs=[FAR] * (len(inputs) + len(small)),
        name="pack",
    )(*(pltpu.with_memory_space_constraint(v, pltpu.HBM) for v in inputs + small))
    fields = results[0]
    owners, vapour_absorption, arid, angle, lit, black, solar = results[1 + packed :]
    if packed:
        homed = lax.all_to_all(results[1], "tile", split_axis=0, concat_axis=0, tiled=True)
    else:
        blocks = factors.reshape(gpoints, n_tile, cap)
        homed = lax.all_to_all(blocks, "tile", split_axis=1, concat_axis=1, tiled=True)
        homed = homed.reshape(gpoints, slots)

    def from_side(distance):
        pairs = []
        for t in range(n_tile):
            for g in range(n_grp):
                s = t - distance if g % 2 == 0 else t + distance
                if 0 <= s < n_tile:
                    pairs.append((s * n_grp + g, t * n_grp + g))
        return lax.ppermute(fields, ("tile", "grp"), pairs)

    def swapped(x, bit):
        return lax.ppermute(x, "grp", [(i, i ^ bit) for i in range(n_grp)])

    near = from_side(1)
    far = from_side(2)
    weights, dry, base = kernel_call(
        functools.partial(gather_kernel, cap, n_tile, packed, levels),
        [(gpoints, width), (levels, gpoints, 128), (stacked, width)],
        name="gather",
    )(homed, owners, vapour_absorption, arid, fields)
    share, mine = kernel_call(
        functools.partial(side_kernel, levels), [(stacked, width)] * 2, name="side"
    )(fields, near, far, base)
    other = swapped(share, 1)
    part, vapour_next, temp = kernel_call(
        functools.partial(radiation_kernel, levels, gpoints),
        [(levels, width), (levels, 1, width), (levels, 1, width)],
        scratch=[
            pltpu.VMEM((levels, gpoints, width), jnp.float32),
            pltpu.VMEM((width // 128, levels * 8, 128), jnp.float32),
        ],
        name="radiation",
    )(mine, other, weights, dry, angle, lit, black, solar)
    bit = 1
    while 2 * bit < n_grp:
        part = part + swapped(part, bit)
        bit *= 2
    heating, temp_next = kernel_call(
        functools.partial(final_kernel, 1.0 / total_g), [(levels, 1, width)] * 2, name="final"
    )(part, swapped(part, bit), temp)
    return heating, temp_next, vapour_next


def solution(mesh):
    in_specs = (
        P(None, "tile", None),
        P(None, "tile", None),
        P("tile", None),
        P("tile", None),
        P("tile", None),
        P("tile", None),
        P("grp", "tile"),
        P("grp", None),
        P("grp"),
        P("grp"),
        P("grp"),
    )
    out_specs = (P(None, "tile", None), P(None, "tile", None), P(None, "tile", None))
    body = functools.partial(on_device, mesh.shape["tile"], mesh.shape["grp"])
    return jax.shard_map(body, mesh=mesh, in_specs=in_specs, out_specs=out_specs, check_vma=False)
```

```python
import functools
import math

import jax
import jax.numpy as jnp
from jax import lax
from jax.experimental import pallas as pl
from jax.experimental.pallas import tpu as pltpu
from jax.sharding import PartitionSpec as P


LOG2E = math.log2(math.e)
VM = pl.BlockSpec(memory_space=pltpu.VMEM)
FAR = pl.BlockSpec(memory_space=pltpu.HBM)


def kernel_call(body, outs, scratch=(), in_specs=None, out_specs=None, flops=1 << 22):
    return pl.pallas_call(
        body,
        out_shape=[o if hasattr(o, "dtype") else jax.ShapeDtypeStruct(o, jnp.float32) for o in outs],
        out_specs=out_specs or [VM] * len(outs),
        scratch_shapes=list(scratch),
        compiler_params=pltpu.CompilerParams(vmem_limit_bytes=24 << 20),
        cost_estimate=pl.CostEstimate(flops=flops, bytes_accessed=1 << 21, transcendentals=0),
        **({} if in_specs is None else {"in_specs": in_specs}),
    )


def split3(x):
    high = x.astype(jnp.bfloat16)
    rest = x - high.astype(jnp.float32)
    middle = rest.astype(jnp.bfloat16)
    low = (rest - middle.astype(jnp.float32)).astype(jnp.bfloat16)
    return high, middle, low


def column_of(row):
    n = row.shape[1]
    r = lax.broadcasted_iota(jnp.int32, (n, n), 0)
    c = lax.broadcasted_iota(jnp.int32, (n, n), 1)
    return jnp.sum(jnp.where(r == c, jnp.broadcast_to(row, (n, n)), 0.0), axis=1, keepdims=True)


def around(v):
    width = v.shape[1]
    return pltpu.roll(v, width - 1, 1) + pltpu.roll(v, 1, 1) - 4.0 * v


def pack_kernel(cap, packed, kept, *refs):
    n_in = kept + 3 + packed
    given, rest = refs[:n_in], refs[n_in:]
    outs, scratch, sems = rest[: 1 + packed + kept], rest[1 + packed + kept : -1], rest[-1]
    targets = tuple(scratch) + tuple(outs[1 + packed :])
    copies = [pltpu.make_async_copy(g, t, sems.at[i]) for i, (g, t) in enumerate(zip(given, targets))]
    for copy in copies:
        copy.start()
    fields = outs[0]
    if packed:
        factors, blocks = scratch[0], outs[1]
        tiles, rows, _ = blocks.shape
        top = factors.shape[0] - rows
        lane = lax.broadcasted_iota(jnp.int32, (rows, 2 * cap), 1)
        copies[0].wait()
        for pair in range(tiles // 2):
            first = factors[0:rows, pair * 2 * cap : (pair + 1) * 2 * cap]
            second = factors[top : top + rows, pair * 2 * cap : (pair + 1) * 2 * cap]
            blocks[2 * pair] = jnp.where(lane < cap, first, pltpu.roll(second, cap, 1))
            blocks[2 * pair + 1] = jnp.where(lane < cap, pltpu.roll(first, cap, 1), second)
    kelvin, moisture, spread = scratch[packed:]
    for copy in copies[packed : packed + 3]:
        copy.wait()
    levels = kelvin.shape[0]
    for l in range(levels):
        fields[l : l + 1, :] = kelvin[l]
        fields[levels + l : levels + l + 1, :] = moisture[l]
    fields[2 * levels : 2 * levels + 1, :] = spread[...]
    left = fields.shape[0] - 2 * levels - 1
    if left:
        fields[2 * levels + 1 :, :] = jnp.zeros((left, fields.shape[1]), jnp.float32)
    for copy in copies[packed + 3 :]:
        copy.wait()


def prepare_kernel(cap, tiles, levels, owners, fields, choice, base):
    columns = owners.shape[1]
    owner = owners[...]
    matches = lax.broadcasted_iota(jnp.int32, (tiles, columns), 0) == owner
    member = matches.astype(jnp.float32)
    r = lax.broadcasted_iota(jnp.int32, (columns, columns), 0)
    c = lax.broadcasted_iota(jnp.int32, (columns, columns), 1)
    earlier = (r < c).astype(jnp.float32).astype(jnp.bfloat16)
    counts = jnp.dot(member.astype(jnp.bfloat16), earlier, preferred_element_type=jnp.float32)
    rank = jnp.sum(jnp.where(matches, counts, 0.0), axis=0, keepdims=True)
    slot = owner * cap + rank.astype(jnp.int32)
    chosen = (lax.broadcasted_iota(jnp.int32, (tiles * cap, columns), 0) == slot).astype(jnp.float32)
    choice[...] = chosen.astype(jnp.bfloat16)
    f = fields[...]
    spread = fields[2 * levels : 2 * levels + 1, :]
    f = f + spread * around(f)
    base[...] = f + spread * around(f)


def select_kernel(cap, tiles, packed, levels, homed, choice, vapour, arid, weights, dry):
    gpoints = weights.shape[0]
    if packed:
        rows = homed.shape[1]
        lane = lax.broadcasted_iota(jnp.int32, (rows, 2 * cap), 1)
        lower, upper = [], []
        for pair in range(tiles // 2):
            first, second = homed[2 * pair], homed[2 * pair + 1]
            lower.append(jnp.where(lane < cap, first, pltpu.roll(second, cap, 1)))
            upper.append(jnp.where(lane < cap, pltpu.roll(first, cap, 1), second))
        lower = jnp.concatenate(lower, axis=1)
        upper = jnp.concatenate(upper, axis=1)[2 * rows - gpoints :]
        table = jnp.concatenate([lower, upper], axis=0)
    else:
        table = homed[...]
    picked = 0.0
    for part in split3(table):
        picked = picked + jnp.dot(part, choice[...], preferred_element_type=jnp.float32)
    weights[...] = picked * (column_of(vapour[...]) * -LOG2E)
    for l in range(levels):
        dry[l] = jnp.broadcast_to(arid[:, l : l + 1] * -LOG2E, (gpoints, dry.shape[2]))


def side_kernel(levels, fields, near, far, base, share, total):
    spread = fields[2 * levels : 2 * levels + 1, :]
    near_spread = near[2 * levels : 2 * levels + 1, :]
    f = near[...]
    near_next = f + near_spread * (far[...] + fields[...] + around(f))
    v = spread * f
    part = v + spread * (around(v) + near_next)
    share[...] = part
    total[...] = base[...] + part


def spread_rows(levels, base, share, temp, wet):
    f = base[...] + share[...]
    for l in range(levels):
        temp[l] = f[l : l + 1]
        wet[l] = f[levels + l : levels + l + 1]


def radiation_kernel(
    levels, gpoints, first, temp, wet, weights, dry, angle, lit, black, solar, part, rest, sums
):
    blocks = gpoints // 8
    black_column = jnp.broadcast_to(column_of(black[...]), (gpoints, 128))
    solar_column = jnp.broadcast_to(column_of(solar[...]), (gpoints, 128))
    unroll = max(u for u in range(1, 11) if levels % u == 0)
    parity = lax.rem(lax.axis_index("grp"), 2)
    half = 1 - parity if first else parity
    at = pl.ds(pl.multiple_of(half * 128, 128), 128)
    mu = jnp.broadcast_to(angle[:, at], (8, 128))
    inverse = 1.0 / mu
    marker = mu * jnp.broadcast_to(lit[:, at].astype(jnp.float32), (8, 128))
    share_of = [black_column[8 * b : 8 * b + 8] for b in range(blocks)]
    weight = [weights[8 * b : 8 * b + 8, at] for b in range(blocks)]
    beams = tuple(solar_column[8 * b : 8 * b + 8] * marker for b in range(blocks))
    zero = tuple(jnp.zeros((8, 128), jnp.float32) for _ in range(blocks))

    def down_level(l, carry):
        down, beam = carry
        warm = jnp.broadcast_to(temp[l, :, at], (8, 128))
        moist = jnp.broadcast_to(wet[l, :, at], (8, 128))
        new_down, new_beam, acc = [], [], None
        for b in range(blocks):
            tau = dry[l, 8 * b : 8 * b + 8, :] + weight[b] * moist
            lost = 1.0 - jnp.exp2(tau)
            rest[l, 8 * b : 8 * b + 8, :] = lost
            step = lost * (down[b] - share_of[b] * warm)
            after = beam[b] * jnp.exp2(tau * inverse)
            net = step + (beam[b] - after)
            acc = net if acc is None else acc + net
            new_down.append(down[b] - step)
            new_beam.append(after)
        sums[pl.ds(pl.multiple_of(l * 8, 8), 8), :] = acc
        return tuple(new_down), tuple(new_beam)

    def up_level(i, up):
        l = levels - 1 - i
        warm = jnp.broadcast_to(temp[l, :, at], (8, 128))
        new_up, acc = [], None
        for b in range(blocks):
            step = rest[l, 8 * b : 8 * b + 8, :] * (share_of[b] * warm - up[b])
            acc = step if acc is None else acc + step
            new_up.append(up[b] + step)
        where = pl.ds(pl.multiple_of(l * 8, 8), 8)
        sums[where, :] = sums[where, :] - acc
        return tuple(new_up)

    lax.fori_loop(0, levels, down_level, (zero, beams), unroll=unroll)
    floor = jnp.broadcast_to(temp[levels - 1, :, at], (8, 128))
    lax.fori_loop(0, levels, up_level, tuple(s * floor for s in share_of), unroll=unroll)
    total = sums[pl.ds(0, levels, stride=8), :]
    for s in range(1, 8):
        total = total + sums[pl.ds(s, levels, stride=8), :]
    part[...] = total


def first_half_kernel(
    levels, gpoints, base, share, weights, dry, angle, lit, black, solar, part, temp, wet, *scratch
):
    spread_rows(levels, base, share, temp, wet)
    radiation_kernel(levels, gpoints, True, temp, wet, weights, dry, angle, lit, black, solar, part, *scratch)


def second_half_kernel(
    levels, gpoints, temp, wet, weights, dry, angle, lit, black, solar, part, vapour, rest, sums, sem
):
    copy = pltpu.make_async_copy(wet, vapour, sem)
    copy.start()
    radiation_kernel(
        levels, gpoints, False, temp, wet, weights, dry, angle, lit, black, solar, part, rest, sums
    )
    copy.wait()


def final_kernel(scale, mine, other, temp, heating, temp_next):
    levels = mine.shape[0]
    even = lax.rem(lax.axis_index("grp"), 2) == 0
    own, far = mine[...] * scale, other[...] * scale
    left, right = jnp.where(even, own, far), jnp.where(even, far, own)
    for at, heat in ((slice(0, 128), left), (slice(128, 256), right)):
        for l in range(levels):
            heating[l, :, at] = heat[l : l + 1]
            temp_next[l, :, at] = temp[l, :, at] + heat[l : l + 1]


def on_device(
    n_tile,
    n_grp,
    kelvin,
    moisture,
    spreading_number,
    angle,
    lit,
    owners,
    factors,
    arid,
    vapour_absorption,
    black,
    solar,
):
    levels, rows, width = kelvin.shape
    gpoints, slots = factors.shape
    cap = slots // n_tile
    total_g = gpoints * n_grp
    if rows != 1 or n_grp & (n_grp - 1) or n_grp < 2 or gpoints % 8 or width != 256:
        raise ValueError("unsupported shapes")
    stacked = -(-(2 * levels + 1) // 8) * 8
    packed = 2 * cap == 128 and gpoints % 16 == 8 and n_tile % 2 == 0
    half = (gpoints + 8) // 2
    inputs = [factors] * packed + [kelvin, moisture, spreading_number]
    row = (1, gpoints)
    small = [owners.reshape(1, width), vapour_absorption.reshape(row), arid]
    small += [angle, lit, black.reshape(row), solar.reshape(row)]
    outs = [jax.ShapeDtypeStruct((stacked, width), jnp.float32)]
    outs += [jax.ShapeDtypeStruct((n_tile, half, 128), jnp.float32)] * packed
    results = kernel_call(
        functools.partial(pack_kernel, cap, packed, len(small)),
        outs + [jax.ShapeDtypeStruct(v.shape, v.dtype) for v in small],
        scratch=[pltpu.VMEM(v.shape, v.dtype) for v in inputs]
        + [pltpu.SemaphoreType.DMA((len(inputs) + len(small),))],
        in_specs=[FAR] * (len(inputs) + len(small)),
    )(*(pltpu.with_memory_space_constraint(v, pltpu.HBM) for v in inputs + small))
    fields = results[0]
    owners, vapour_absorption, arid, angle, lit, black, solar = results[1 + packed :]
    if packed:
        homed = lax.all_to_all(results[1], "tile", split_axis=0, concat_axis=0, tiled=True)
    else:
        blocks = factors.reshape(gpoints, n_tile, cap)
        homed = lax.all_to_all(blocks, "tile", split_axis=1, concat_axis=1, tiled=True)
        homed = homed.reshape(gpoints, slots)

    def from_side(distance):
        pairs = []
        for t in range(n_tile):
            for g in range(n_grp):
                s = t - distance if g % 2 == 0 else t + distance
                if 0 <= s < n_tile:
                    pairs.append((s * n_grp + g, t * n_grp + g))
        return lax.ppermute(fields, ("tile", "grp"), pairs)

    def swapped(x, bit):
        return lax.ppermute(x, "grp", [(i, i ^ bit) for i in range(n_grp)])

    near = from_side(1)
    far = from_side(2)
    choice, base = kernel_call(
        functools.partial(prepare_kernel, cap, n_tile, levels),
        [jax.ShapeDtypeStruct((slots, width), jnp.bfloat16), (stacked, width)],
    )(owners, fields)
    weights, dry = kernel_call(
        functools.partial(select_kernel, cap, n_tile, packed, levels),
        [(gpoints, width), (levels, gpoints, 128)],
    )(homed, choice, vapour_absorption, arid)
    share, mine = kernel_call(
        functools.partial(side_kernel, levels), [(stacked, width)] * 2
    )(fields, near, far, base)
    other = swapped(share, 1)
    tables = (weights, dry, angle, lit, black, solar)
    work = [
        pltpu.VMEM((levels, gpoints, 128), jnp.float32),
        pltpu.VMEM((levels * 8, 128), jnp.float32),
    ]
    given, temp, wet = kernel_call(
        functools.partial(first_half_kernel, levels, gpoints),
        [(levels, 128), (levels, 1, width), (levels, 1, width)],
        scratch=work,
    )(mine, other, *tables)
    taken = swapped(given, 1)
    part, vapour_next = kernel_call(
        functools.partial(second_half_kernel, levels, gpoints),
        [(levels, 128), (levels, 1, width)],
        scratch=work + [pltpu.SemaphoreType.DMA],
        out_specs=[VM, FAR],
    )(temp, wet, *tables)
    part = part + taken
    bit = 2
    while bit < n_grp:
        part = part + swapped(part, bit)
        bit *= 2
    heating, temp_next = kernel_call(
        functools.partial(final_kernel, 1.0 / total_g), [(levels, 1, width)] * 2
    )(part, swapped(part, 1), temp)
    return heating, temp_next, vapour_next


def solution(mesh):
    in_specs = (
        P(None, "tile", None),
        P(None, "tile", None),
        P("tile", None),
        P("tile", None),
        P("tile", None),
        P("tile", None),
        P("grp", "tile"),
        P("grp", None),
        P("grp"),
        P("grp"),
        P("grp"),
    )
    out_specs = (P(None, "tile", None), P(None, "tile", None), P(None, "tile", None))

    def body(*args):
        return on_device(mesh.shape["tile"], mesh.shape["grp"], *args)

    return jax.shard_map(body, mesh=mesh, in_specs=in_specs, out_specs=out_specs, check_vma=False)
```

```python
import functools
import math

import jax
import jax.numpy as jnp
from jax import lax
from jax.experimental import pallas as pl
from jax.experimental.pallas import tpu as pltpu
from jax.sharding import PartitionSpec as P


LOG2E = math.log2(math.e)
VM = pl.BlockSpec(memory_space=pltpu.VMEM)
FAR = pl.BlockSpec(memory_space=pltpu.HBM)


def kernel_call(body, outs, scratch=(), in_specs=None, out_specs=None, flops=1 << 22):
    return pl.pallas_call(
        body,
        out_shape=[o if hasattr(o, "dtype") else jax.ShapeDtypeStruct(o, jnp.float32) for o in outs],
        out_specs=out_specs or [VM] * len(outs),
        scratch_shapes=list(scratch),
        compiler_params=pltpu.CompilerParams(vmem_limit_bytes=24 << 20),
        cost_estimate=pl.CostEstimate(flops=flops, bytes_accessed=1 << 21, transcendentals=0),
        **({} if in_specs is None else {"in_specs": in_specs}),
    )


def split3(x):
    high = x.astype(jnp.bfloat16)
    rest = x - high.astype(jnp.float32)
    middle = rest.astype(jnp.bfloat16)
    low = (rest - middle.astype(jnp.float32)).astype(jnp.bfloat16)
    return high, middle, low


def column_of(row):
    n = row.shape[1]
    r = lax.broadcasted_iota(jnp.int32, (n, n), 0)
    c = lax.broadcasted_iota(jnp.int32, (n, n), 1)
    return jnp.sum(jnp.where(r == c, jnp.broadcast_to(row, (n, n)), 0.0), axis=1, keepdims=True)


def around(v):
    width = v.shape[1]
    return pltpu.roll(v, width - 1, 1) + pltpu.roll(v, 1, 1) - 4.0 * v


def pack_kernel(cap, packed, kept, *refs):
    n_in = kept + 3 + packed
    given, rest = refs[:n_in], refs[n_in:]
    outs, scratch, sems = rest[: 1 + packed + kept], rest[1 + packed + kept : -1], rest[-1]
    scratch, spare = scratch[: 3 + packed], scratch[3 + packed :]
    targets = tuple(scratch) + tuple(outs[1 + packed :])
    copies = [pltpu.make_async_copy(g, t, sems.at[i]) for i, (g, t) in enumerate(zip(given, targets))]
    for copy in copies:
        copy.start()
    fields = outs[0]
    if packed:
        factors, blocks = scratch[0], spare[0]
        tiles, rows, _ = blocks.shape
        top = factors.shape[0] - rows
        lane = lax.broadcasted_iota(jnp.int32, (rows, 2 * cap), 1)
        copies[0].wait()
        for pair in range(tiles // 2):
            first = factors[0:rows, pair * 2 * cap : (pair + 1) * 2 * cap]
            second = factors[top : top + rows, pair * 2 * cap : (pair + 1) * 2 * cap]
            blocks[2 * pair] = jnp.where(lane < cap, first, pltpu.roll(second, cap, 1))
            blocks[2 * pair + 1] = jnp.where(lane < cap, pltpu.roll(first, cap, 1), second)
        sending = pltpu.make_async_copy(blocks, outs[1], sems.at[n_in])
        sending.start()
    kelvin, moisture, spread = scratch[packed:]
    for copy in copies[packed : packed + 3]:
        copy.wait()
    levels = kelvin.shape[0]
    for l in range(levels):
        fields[l : l + 1, :] = kelvin[l]
        fields[levels + l : levels + l + 1, :] = moisture[l]
    fields[2 * levels : 2 * levels + 1, :] = spread[...]
    left = fields.shape[0] - 2 * levels - 1
    if left:
        fields[2 * levels + 1 :, :] = jnp.zeros((left, fields.shape[1]), jnp.float32)
    for copy in copies[packed + 3 :]:
        copy.wait()
    if packed:
        sending.wait()


def prepare_kernel(cap, tiles, levels, fields, *refs):
    given, (slot, dry, base), kept, (owners, arid, sems) = refs[:7], refs[7:10], refs[10:15], refs[15:]
    copies = [
        pltpu.make_async_copy(g, t, sems.at[i]) for i, (g, t) in enumerate(zip(given, (owners, arid) + kept))
    ]
    for copy in copies:
        copy.start()
    f = fields[...]
    spread = fields[2 * levels : 2 * levels + 1, :]
    f = f + spread * around(f)
    base[...] = f + spread * around(f)
    for copy in copies:
        copy.wait()
    columns = owners.shape[1]
    gpoints = arid.shape[0]
    owner = owners[...]
    matches = lax.broadcasted_iota(jnp.int32, (tiles, columns), 0) == owner
    member = matches.astype(jnp.float32)
    r = lax.broadcasted_iota(jnp.int32, (columns, columns), 0)
    c = lax.broadcasted_iota(jnp.int32, (columns, columns), 1)
    earlier = (r < c).astype(jnp.float32).astype(jnp.bfloat16)
    counts = jnp.dot(member.astype(jnp.bfloat16), earlier, preferred_element_type=jnp.float32)
    rank = jnp.sum(jnp.where(matches, counts, 0.0), axis=0, keepdims=True)
    slot[...] = owner * cap + rank.astype(jnp.int32)
    for l in range(levels):
        dry[l] = jnp.broadcast_to(arid[:, l : l + 1] * -LOG2E, (gpoints, dry.shape[2]))


def select_kernel(cap, tiles, packed, homed, slot, vapour, weights):
    gpoints = weights.shape[0]
    if packed:
        rows = homed.shape[1]
        lane = lax.broadcasted_iota(jnp.int32, (rows, 2 * cap), 1)
        lower, upper = [], []
        for pair in range(tiles // 2):
            first, second = homed[2 * pair], homed[2 * pair + 1]
            lower.append(jnp.where(lane < cap, first, pltpu.roll(second, cap, 1)))
            upper.append(jnp.where(lane < cap, pltpu.roll(first, cap, 1), second))
        lower = jnp.concatenate(lower, axis=1)
        upper = jnp.concatenate(upper, axis=1)[2 * rows - gpoints :]
        table = jnp.concatenate([lower, upper], axis=0)
    else:
        table = homed[...]
    chosen = lax.broadcasted_iota(jnp.int32, (tiles * cap, slot.shape[1]), 0) == slot[...]
    choice = chosen.astype(jnp.float32).astype(jnp.bfloat16)
    picked = 0.0
    for part in split3(table):
        picked = picked + jnp.dot(part, choice, preferred_element_type=jnp.float32)
    weights[...] = picked * (column_of(vapour[...]) * -LOG2E)


def side_kernel(levels, fields, near, far, base, share, total):
    spread = fields[2 * levels : 2 * levels + 1, :]
    near_spread = near[2 * levels : 2 * levels + 1, :]
    f = near[...]
    near_next = f + near_spread * (far[...] + fields[...] + around(f))
    v = spread * f
    part = v + spread * (around(v) + near_next)
    share[...] = part
    total[...] = base[...] + part


def spread_rows(levels, base, share, temp, wet):
    f = base[...] + share[...]
    for l in range(levels):
        temp[l] = f[l : l + 1]
        wet[l] = f[levels + l : levels + l + 1]


def tree_sum(terms):
    terms = list(terms)
    while len(terms) > 1:
        terms = [sum(terms[i + 1 : i + 2], terms[i]) for i in range(0, len(terms), 2)]
    return terms[0]


def unrolled(levels, most):
    return max(u for u in range(1, most + 1) if levels % u == 0)


UD, UU = 30, 90


def radiation_kernel(
    levels, gpoints, first, temp, wet, weights, dry, angle, lit, black, solar, part, rest, steps, sums
):
    blocks = gpoints // 8
    black_column = jnp.broadcast_to(column_of(black[...]), (gpoints, 128))
    solar_column = jnp.broadcast_to(column_of(solar[...]), (gpoints, 128))
    parity = lax.rem(lax.axis_index("grp"), 2)
    half = 1 - parity if first else parity
    at = pl.ds(pl.multiple_of(half * 128, 128), 128)
    mu = jnp.broadcast_to(angle[:, at], (8, 128))
    inverse = 1.0 / mu
    marker = mu * jnp.broadcast_to(lit[:, at].astype(jnp.float32), (8, 128))
    share_of = [black_column[8 * b : 8 * b + 8] for b in range(blocks)]
    weight = [weights[8 * b : 8 * b + 8, at] for b in range(blocks)]
    beams = tuple(solar_column[8 * b : 8 * b + 8] * marker for b in range(blocks))
    zero = jnp.zeros((8, 128), jnp.float32)

    def level(l):
        return pl.ds(pl.multiple_of(l * 8, 8), 8)

    def down_level(l, carry):
        down, beam, passed = carry
        warm = jnp.broadcast_to(temp[l, :, at], (8, 128))
        moist = jnp.broadcast_to(wet[l, :, at], (8, 128))
        new_down, new_beam = [], []
        for b in range(blocks):
            tau = dry[l, 8 * b : 8 * b + 8, :] + weight[b] * moist
            lost = 1.0 - jnp.exp2(tau)
            step = lost * (down[b] - warm)
            rest[l, 8 * b : 8 * b + 8, :] = lost
            steps[l, 8 * b : 8 * b + 8, :] = step
            after = beam[b] * jnp.exp2(tau * inverse)
            new_down.append(down[b] - step)
            new_beam.append(after)
        passing = tree_sum(new_beam)
        sums[level(l), :] = passed - passing
        return tuple(new_down), tuple(new_beam), passing

    def up_level(i, up):
        l = levels - 1 - i
        warm = jnp.broadcast_to(temp[l, :, at], (8, 128))
        new_up, terms = [], [sums[level(l), :]]
        for b in range(blocks):
            step = rest[l, 8 * b : 8 * b + 8, :] * (up[b] - warm)
            terms.append(share_of[b] * (step + steps[l, 8 * b : 8 * b + 8, :]))
            new_up.append(up[b] - step)
        sums[level(l), :] = tree_sum(terms)
        return tuple(new_up)

    lax.fori_loop(0, levels, down_level, ((zero,) * blocks, beams, tree_sum(beams)), unroll=unrolled(levels, UD))
    floor = jnp.broadcast_to(temp[levels - 1, :, at], (8, 128))
    lax.fori_loop(0, levels, up_level, (floor,) * blocks, unroll=unrolled(levels, UU))
    total = sums[pl.ds(0, levels, stride=8), :]
    for s in range(1, 8):
        total = total + sums[pl.ds(s, levels, stride=8), :]
    part[...] = total


def first_half_kernel(
    levels, gpoints, base, share, weights, dry, angle, lit, black, solar, part, temp, wet, *scratch
):
    spread_rows(levels, base, share, temp, wet)
    radiation_kernel(levels, gpoints, True, temp, wet, weights, dry, angle, lit, black, solar, part, *scratch)


def second_half_kernel(
    levels, gpoints, temp, wet, weights, dry, angle, lit, black, solar, part, vapour, rest, steps, sums, sem
):
    copy = pltpu.make_async_copy(wet, vapour, sem)
    copy.start()
    radiation_kernel(
        levels, gpoints, False, temp, wet, weights, dry, angle, lit, black, solar, part, rest, steps, sums
    )
    copy.wait()


def final_kernel(scale, mine, other, temp, heating, temp_next):
    levels = mine.shape[0]
    even = lax.rem(lax.axis_index("grp"), 2) == 0
    own, far = mine[...] * scale, other[...] * scale
    left, right = jnp.where(even, own, far), jnp.where(even, far, own)
    for at, heat in ((slice(0, 128), left), (slice(128, 256), right)):
        for l in range(levels):
            heating[l, :, at] = heat[l : l + 1]
            temp_next[l, :, at] = temp[l, :, at] + heat[l : l + 1]


def on_device(
    n_tile,
    n_grp,
    kelvin,
    moisture,
    spreading_number,
    angle,
    lit,
    owners,
    factors,
    arid,
    vapour_absorption,
    black,
    solar,
):
    levels, rows, width = kelvin.shape
    gpoints, slots = factors.shape
    cap = slots // n_tile
    total_g = gpoints * n_grp
    if rows != 1 or n_grp & (n_grp - 1) or n_grp < 2 or gpoints % 8 or width != 256:
        raise ValueError("unsupported shapes")
    stacked = -(-(2 * levels + 1) // 8) * 8
    packed = 2 * cap == 128 and gpoints % 16 == 8 and n_tile % 2 == 0
    half = (gpoints + 8) // 2
    inputs = [factors] * packed + [kelvin, moisture, spreading_number]
    row = (1, gpoints)
    small = [owners.reshape(1, width), arid, vapour_absorption.reshape(row)]
    small += [angle, lit, black.reshape(row), solar.reshape(row)]
    outs = [jax.ShapeDtypeStruct((stacked, width), jnp.float32)]
    outs += [jax.ShapeDtypeStruct((n_tile, half, 128), jnp.float32)] * packed
    results = kernel_call(
        functools.partial(pack_kernel, cap, packed, 0),
        outs,
        scratch=[pltpu.VMEM(v.shape, v.dtype) for v in inputs]
        + [pltpu.VMEM((n_tile, half, 128), jnp.float32)] * packed
        + [pltpu.SemaphoreType.DMA((len(inputs) + packed,))],
        in_specs=[FAR] * len(inputs),
        out_specs=[VM] + [FAR] * packed,
    )(*(pltpu.with_memory_space_constraint(v, pltpu.HBM) for v in inputs))
    fields = results[0]
    if packed:
        homed = lax.all_to_all(results[1], "tile", split_axis=0, concat_axis=0, tiled=True)
    else:
        blocks = factors.reshape(gpoints, n_tile, cap)
        homed = lax.all_to_all(blocks, "tile", split_axis=1, concat_axis=1, tiled=True)
        homed = homed.reshape(gpoints, slots)

    def from_side(distance):
        pairs = []
        for t in range(n_tile):
            for g in range(n_grp):
                s = t - distance if g % 2 == 0 else t + distance
                if 0 <= s < n_tile:
                    pairs.append((s * n_grp + g, t * n_grp + g))
        return lax.ppermute(fields, ("tile", "grp"), pairs)

    def swapped(x, bit):
        return lax.ppermute(x, "grp", [(i, i ^ bit) for i in range(n_grp)])

    near = from_side(1)
    far = from_side(2)
    slot, dry, base, vapour_absorption, angle, lit, black, solar = kernel_call(
        functools.partial(prepare_kernel, cap, n_tile, levels),
        [jax.ShapeDtypeStruct((1, width), jnp.int32), (levels, gpoints, 128), (stacked, width)]
        + [jax.ShapeDtypeStruct(v.shape, v.dtype) for v in small[2:]],
        scratch=[pltpu.VMEM(v.shape, v.dtype) for v in small[:2]]
        + [pltpu.SemaphoreType.DMA((len(small),))],
        in_specs=[VM] + [FAR] * len(small),
    )(fields, *(pltpu.with_memory_space_constraint(v, pltpu.HBM) for v in small))
    (weights,) = kernel_call(
        functools.partial(select_kernel, cap, n_tile, packed), [(gpoints, width)]
    )(homed, slot, vapour_absorption)
    share, mine = kernel_call(functools.partial(side_kernel, levels), [(stacked, width)] * 2)(fields, near, far, base)
    other = swapped(share, 1)
    tables = (weights, dry, angle, lit, black, solar)
    work = [
        pltpu.VMEM((levels, gpoints, 128), jnp.float32),
        pltpu.VMEM((levels, gpoints, 128), jnp.float32),
        pltpu.VMEM((levels * 8, 128), jnp.float32),
    ]
    given, temp, wet = kernel_call(
        functools.partial(first_half_kernel, levels, gpoints),
        [(levels, 128), (levels, 1, width), (levels, 1, width)],
        scratch=work,
    )(mine, other, *tables)
    taken = swapped(given, 1)
    part, vapour_next = kernel_call(
        functools.partial(second_half_kernel, levels, gpoints),
        [(levels, 128), (levels, 1, width)],
        scratch=work + [pltpu.SemaphoreType.DMA],
        out_specs=[VM, FAR],
    )(temp, wet, *tables)
    part = part + taken
    bit = 2
    while bit < n_grp:
        part = part + swapped(part, bit)
        bit *= 2
    heating, temp_next = kernel_call(
        functools.partial(final_kernel, 1.0 / total_g), [(levels, 1, width)] * 2
    )(part, swapped(part, 1), temp)
    return heating, temp_next, vapour_next


def solution(mesh):
    in_specs = (
        P(None, "tile", None),
        P(None, "tile", None),
        P("tile", None),
        P("tile", None),
        P("tile", None),
        P("tile", None),
        P("grp", "tile"),
        P("grp", None),
        P("grp"),
        P("grp"),
        P("grp"),
    )
    out_specs = (P(None, "tile", None), P(None, "tile", None), P(None, "tile", None))

    def body(*args):
        return on_device(mesh.shape["tile"], mesh.shape["grp"], *args)

    return jax.shard_map(body, mesh=mesh, in_specs=in_specs, out_specs=out_specs, check_vma=False)
```

```python
import functools
import math

import jax
import jax.numpy as jnp
from jax import lax
from jax.experimental import pallas as pl
from jax.experimental.pallas import tpu as pltpu
from jax.sharding import PartitionSpec as P


LOG2E = math.log2(math.e)
VM = pl.BlockSpec(memory_space=pltpu.VMEM)
FAR = pl.BlockSpec(memory_space=pltpu.HBM)


def kernel_call(body, outs, scratch=(), in_specs=None, out_specs=None, flops=1 << 22):
    return pl.pallas_call(
        body,
        out_shape=[o if hasattr(o, "dtype") else jax.ShapeDtypeStruct(o, jnp.float32) for o in outs],
        out_specs=out_specs or [VM] * len(outs),
        scratch_shapes=list(scratch),
        compiler_params=pltpu.CompilerParams(vmem_limit_bytes=24 << 20),
        cost_estimate=pl.CostEstimate(flops=flops, bytes_accessed=1 << 21, transcendentals=0),
        **({} if in_specs is None else {"in_specs": in_specs}),
    )


def split3(x):
    high = x.astype(jnp.bfloat16)
    rest = x - high.astype(jnp.float32)
    middle = rest.astype(jnp.bfloat16)
    low = (rest - middle.astype(jnp.float32)).astype(jnp.bfloat16)
    return high, middle, low


def column_of(row):
    n = row.shape[1]
    r = lax.broadcasted_iota(jnp.int32, (n, n), 0)
    c = lax.broadcasted_iota(jnp.int32, (n, n), 1)
    return jnp.sum(jnp.where(r == c, jnp.broadcast_to(row, (n, n)), 0.0), axis=1, keepdims=True)


def around(v):
    width = v.shape[1]
    return pltpu.roll(v, width - 1, 1) + pltpu.roll(v, 1, 1) - 4.0 * v


def pack_kernel(cap, packed, kept, *refs):
    n_in = kept + 3 + packed
    given, rest = refs[:n_in], refs[n_in:]
    outs, scratch, sems = rest[: 1 + packed + kept], rest[1 + packed + kept : -1], rest[-1]
    scratch, spare = scratch[: 3 + packed], scratch[3 + packed :]
    targets = tuple(scratch) + tuple(outs[1 + packed :])
    copies = [pltpu.make_async_copy(g, t, sems.at[i]) for i, (g, t) in enumerate(zip(given, targets))]
    for copy in copies:
        copy.start()
    fields = outs[0]
    if packed:
        factors, blocks = scratch[0], spare[0]
        tiles, rows, _ = blocks.shape
        top = factors.shape[0] - rows
        lane = lax.broadcasted_iota(jnp.int32, (rows, 2 * cap), 1)
        copies[0].wait()
        for pair in range(tiles // 2):
            first = factors[0:rows, pair * 2 * cap : (pair + 1) * 2 * cap]
            second = factors[top : top + rows, pair * 2 * cap : (pair + 1) * 2 * cap]
            blocks[2 * pair] = jnp.where(lane < cap, first, pltpu.roll(second, cap, 1))
            blocks[2 * pair + 1] = jnp.where(lane < cap, pltpu.roll(first, cap, 1), second)
        sending = pltpu.make_async_copy(blocks, outs[1], sems.at[n_in])
        sending.start()
    kelvin, moisture, spread = scratch[packed:]
    for copy in copies[packed : packed + 3]:
        copy.wait()
    levels = kelvin.shape[0]
    for l in range(levels):
        fields[l : l + 1, :] = kelvin[l]
        fields[levels + l : levels + l + 1, :] = moisture[l]
    fields[2 * levels : 2 * levels + 1, :] = spread[...]
    left = fields.shape[0] - 2 * levels - 1
    if left:
        fields[2 * levels + 1 :, :] = jnp.zeros((left, fields.shape[1]), jnp.float32)
    for copy in copies[packed + 3 :]:
        copy.wait()
    if packed:
        sending.wait()


def prepare_kernel(cap, tiles, levels, fields, near, *refs):
    given, (slot, dry, base, part), kept, (owners, arid, sems) = refs[:7], refs[7:11], refs[11:16], refs[16:]
    copies = [
        pltpu.make_async_copy(g, t, sems.at[i]) for i, (g, t) in enumerate(zip(given, (owners, arid) + kept))
    ]
    for copy in copies:
        copy.start()
    f = fields[...]
    spread = fields[2 * levels : 2 * levels + 1, :]
    first = f + spread * around(f)
    n = near[...]
    v = spread * n
    side = v + spread * (around(v) + n + near[2 * levels : 2 * levels + 1, :] * (f + around(n)))
    part[...] = side
    base[...] = first + spread * around(first) + side
    for copy in copies:
        copy.wait()
    columns = owners.shape[1]
    gpoints = arid.shape[0]
    owner = owners[...]
    matches = lax.broadcasted_iota(jnp.int32, (tiles, columns), 0) == owner
    member = matches.astype(jnp.float32)
    r = lax.broadcasted_iota(jnp.int32, (columns, columns), 0)
    c = lax.broadcasted_iota(jnp.int32, (columns, columns), 1)
    earlier = (r < c).astype(jnp.float32).astype(jnp.bfloat16)
    counts = jnp.dot(member.astype(jnp.bfloat16), earlier, preferred_element_type=jnp.float32)
    rank = jnp.sum(jnp.where(matches, counts, 0.0), axis=0, keepdims=True)
    slot[...] = owner * cap + rank.astype(jnp.int32)
    for l in range(levels):
        dry[l] = jnp.broadcast_to(arid[:, l : l + 1] * -LOG2E, (gpoints, dry.shape[2]))


def select_kernel(cap, tiles, packed, homed, slot, vapour, weights):
    gpoints = weights.shape[0]
    if packed:
        rows = homed.shape[1]
        lane = lax.broadcasted_iota(jnp.int32, (rows, 2 * cap), 1)
        lower, upper = [], []
        for pair in range(tiles // 2):
            first, second = homed[2 * pair], homed[2 * pair + 1]
            lower.append(jnp.where(lane < cap, first, pltpu.roll(second, cap, 1)))
            upper.append(jnp.where(lane < cap, pltpu.roll(first, cap, 1), second))
        lower = jnp.concatenate(lower, axis=1)
        upper = jnp.concatenate(upper, axis=1)[2 * rows - gpoints :]
        table = jnp.concatenate([lower, upper], axis=0)
    else:
        table = homed[...]
    chosen = lax.broadcasted_iota(jnp.int32, (tiles * cap, slot.shape[1]), 0) == slot[...]
    choice = chosen.astype(jnp.float32).astype(jnp.bfloat16)
    picked = 0.0
    for part in split3(table):
        picked = picked + jnp.dot(part, choice, preferred_element_type=jnp.float32)
    weights[...] = picked * (column_of(vapour[...]) * -LOG2E)


def side_kernel(levels, fields, near, far, base, part, share, total):
    row = slice(2 * levels, 2 * levels + 1)
    add = (fields[row, :] * near[row, :]) * far[...]
    share[...] = part[...] + add
    total[...] = base[...] + add


def spread_rows(levels, base, share, temp, wet):
    f = base[...] + share[...]
    for l in range(levels):
        temp[l] = f[l : l + 1]
        wet[l] = f[levels + l : levels + l + 1]


def tree_sum(terms):
    terms = list(terms)
    while len(terms) > 1:
        terms = [sum(terms[i + 1 : i + 2], terms[i]) for i in range(0, len(terms), 2)]
    return terms[0]


def unrolled(levels, most):
    return max(u for u in range(1, most + 1) if levels % u == 0)


UD, UU = 30, 90


def radiation_kernel(
    levels, gpoints, first, temp, wet, weights, dry, angle, lit, black, solar, part, rest, steps, sums
):
    blocks = gpoints // 8
    black_column = jnp.broadcast_to(column_of(black[...]), (gpoints, 128))
    solar_column = jnp.broadcast_to(column_of(solar[...]), (gpoints, 128))
    parity = lax.rem(lax.axis_index("grp"), 2)
    half = 1 - parity if first else parity
    at = pl.ds(pl.multiple_of(half * 128, 128), 128)
    mu = jnp.broadcast_to(angle[:, at], (8, 128))
    inverse = 1.0 / mu
    marker = mu * jnp.broadcast_to(lit[:, at].astype(jnp.float32), (8, 128))
    share_of = [black_column[8 * b : 8 * b + 8] for b in range(blocks)]
    weight = [weights[8 * b : 8 * b + 8, at] for b in range(blocks)]
    beams = tuple(solar_column[8 * b : 8 * b + 8] * marker for b in range(blocks))
    zero = jnp.zeros((8, 128), jnp.float32)

    def level(l):
        return pl.ds(pl.multiple_of(l * 8, 8), 8)

    def down_level(l, carry):
        down, beam = carry
        warm = jnp.broadcast_to(temp[l, :, at], (8, 128))
        moist = jnp.broadcast_to(wet[l, :, at], (8, 128))
        sums[level(l), :] = tree_sum(beam)
        new_down, new_beam = [], []
        for b in range(blocks):
            tau = dry[l, 8 * b : 8 * b + 8, :] + weight[b] * moist
            kept = jnp.exp2(tau)
            rest[l, 8 * b : 8 * b + 8, :] = kept
            steps[l, 8 * b : 8 * b + 8, :] = down[b]
            new_beam.append(beam[b] * jnp.exp2(tau * inverse))
            new_down.append(warm + kept * (down[b] - warm))
        return tuple(new_down), tuple(new_beam)

    def up_level(i, carry):
        up, below = carry
        l = levels - 1 - i
        warm = jnp.broadcast_to(temp[l, :, at], (8, 128))
        new_up, terms = [], [sums[level(l), :]]
        for b in range(blocks):
            u = warm + rest[l, 8 * b : 8 * b + 8, :] * (up[b] - warm)
            terms.append(share_of[b] * (steps[l, 8 * b : 8 * b + 8, :] - u))
            new_up.append(u)
        flux = tree_sum(terms)
        sums[level(l), :] = flux - below
        return tuple(new_up), flux

    down, beam = lax.fori_loop(
        0, levels, down_level, ((zero,) * blocks, beams), unroll=unrolled(levels, UD)
    )
    floor = jnp.broadcast_to(temp[levels - 1, :, at], (8, 128))
    ground = tree_sum([s * (d - floor) for s, d in zip(share_of, down)] + list(beam))
    lax.fori_loop(0, levels, up_level, ((floor,) * blocks, ground), unroll=unrolled(levels, UU))
    total = sums[pl.ds(0, levels, stride=8), :]
    for s in range(1, 8):
        total = total + sums[pl.ds(s, levels, stride=8), :]
    part[...] = total


def first_half_kernel(
    levels, gpoints, base, share, weights, dry, angle, lit, black, solar, part, temp, wet, *scratch
):
    spread_rows(levels, base, share, temp, wet)
    radiation_kernel(levels, gpoints, True, temp, wet, weights, dry, angle, lit, black, solar, part, *scratch)


def second_half_kernel(
    levels, gpoints, temp, wet, weights, dry, angle, lit, black, solar, part, vapour, rest, steps, sums, sem
):
    copy = pltpu.make_async_copy(wet, vapour, sem)
    copy.start()
    radiation_kernel(
        levels, gpoints, False, temp, wet, weights, dry, angle, lit, black, solar, part, rest, steps, sums
    )
    copy.wait()


def final_kernel(scale, mine, other, temp, heating, temp_next):
    levels = mine.shape[0]
    even = lax.rem(lax.axis_index("grp"), 2) == 0
    own, far = mine[...] * scale, other[...] * scale
    left, right = jnp.where(even, own, far), jnp.where(even, far, own)
    for at, heat in ((slice(0, 128), left), (slice(128, 256), right)):
        for l in range(levels):
            heating[l, :, at] = heat[l : l + 1]
            temp_next[l, :, at] = temp[l, :, at] + heat[l : l + 1]


def on_device(
    n_tile,
    n_grp,
    kelvin,
    moisture,
    spreading_number,
    angle,
    lit,
    owners,
    factors,
    arid,
    vapour_absorption,
    black,
    solar,
):
    levels, rows, width = kelvin.shape
    gpoints, slots = factors.shape
    cap = slots // n_tile
    total_g = gpoints * n_grp
    if rows != 1 or n_grp & (n_grp - 1) or n_grp < 2 or gpoints % 8 or width != 256:
        raise ValueError("unsupported shapes")
    stacked = -(-(2 * levels + 1) // 8) * 8
    packed = 2 * cap == 128 and gpoints % 16 == 8 and n_tile % 2 == 0
    half = (gpoints + 8) // 2
    inputs = [factors] * packed + [kelvin, moisture, spreading_number]
    row = (1, gpoints)
    small = [owners.reshape(1, width), arid, vapour_absorption.reshape(row)]
    small += [angle, lit, black.reshape(row), solar.reshape(row)]
    outs = [jax.ShapeDtypeStruct((stacked, width), jnp.float32)]
    outs += [jax.ShapeDtypeStruct((n_tile, half, 128), jnp.float32)] * packed
    results = kernel_call(
        functools.partial(pack_kernel, cap, packed, 0),
        outs,
        scratch=[pltpu.VMEM(v.shape, v.dtype) for v in inputs]
        + [pltpu.VMEM((n_tile, half, 128), jnp.float32)] * packed
        + [pltpu.SemaphoreType.DMA((len(inputs) + packed,))],
        in_specs=[FAR] * len(inputs),
        out_specs=[VM] + [FAR] * packed,
    )(*(pltpu.with_memory_space_constraint(v, pltpu.HBM) for v in inputs))
    fields = results[0]
    if packed:
        homed = lax.all_to_all(results[1], "tile", split_axis=0, concat_axis=0, tiled=True)
    else:
        blocks = factors.reshape(gpoints, n_tile, cap)
        homed = lax.all_to_all(blocks, "tile", split_axis=1, concat_axis=1, tiled=True)
        homed = homed.reshape(gpoints, slots)

    def from_side(distance):
        pairs = []
        for t in range(n_tile):
            for g in range(n_grp):
                s = t - distance if g % 2 == 0 else t + distance
                if 0 <= s < n_tile:
                    pairs.append((s * n_grp + g, t * n_grp + g))
        return lax.ppermute(fields, ("tile", "grp"), pairs)

    def swapped(x, bit):
        return lax.ppermute(x, "grp", [(i, i ^ bit) for i in range(n_grp)])

    near = from_side(1)
    far = from_side(2)
    slot, dry, base, side, vapour_absorption, angle, lit, black, solar = kernel_call(
        functools.partial(prepare_kernel, cap, n_tile, levels),
        [jax.ShapeDtypeStruct((1, width), jnp.int32), (levels, gpoints, 128)]
        + [(stacked, width)] * 2
        + [jax.ShapeDtypeStruct(v.shape, v.dtype) for v in small[2:]],
        scratch=[pltpu.VMEM(v.shape, v.dtype) for v in small[:2]]
        + [pltpu.SemaphoreType.DMA((len(small),))],
        in_specs=[VM] * 2 + [FAR] * len(small),
    )(fields, near, *(pltpu.with_memory_space_constraint(v, pltpu.HBM) for v in small))
    (weights,) = kernel_call(
        functools.partial(select_kernel, cap, n_tile, packed), [(gpoints, width)]
    )(homed, slot, vapour_absorption)
    share, mine = kernel_call(
        functools.partial(side_kernel, levels), [(stacked, width)] * 2
    )(fields, near, far, base, side)
    other = swapped(share, 1)
    tables = (weights, dry, angle, lit, black, solar)
    work = [
        pltpu.VMEM((levels, gpoints, 128), jnp.float32),
        pltpu.VMEM((levels, gpoints, 128), jnp.float32),
        pltpu.VMEM((levels * 8, 128), jnp.float32),
    ]
    given, temp, wet = kernel_call(
        functools.partial(first_half_kernel, levels, gpoints),
        [(levels, 128), (levels, 1, width), (levels, 1, width)],
        scratch=work,
    )(mine, other, *tables)
    taken = swapped(given, 1)
    part, vapour_next = kernel_call(
        functools.partial(second_half_kernel, levels, gpoints),
        [(levels, 128), (levels, 1, width)],
        scratch=work + [pltpu.SemaphoreType.DMA],
        out_specs=[VM, FAR],
    )(temp, wet, *tables)
    part = part + taken
    bit = 2
    while bit < n_grp:
        part = part + swapped(part, bit)
        bit *= 2
    heating, temp_next = kernel_call(
        functools.partial(final_kernel, 1.0 / total_g), [(levels, 1, width)] * 2
    )(part, swapped(part, 1), temp)
    return heating, temp_next, vapour_next


def solution(mesh):
    in_specs = (
        P(None, "tile", None),
        P(None, "tile", None),
        P("tile", None),
        P("tile", None),
        P("tile", None),
        P("tile", None),
        P("grp", "tile"),
        P("grp", None),
        P("grp"),
        P("grp"),
        P("grp"),
    )
    out_specs = (P(None, "tile", None), P(None, "tile", None), P(None, "tile", None))

    def body(*args):
        return on_device(mesh.shape["tile"], mesh.shape["grp"], *args)

    return jax.shard_map(body, mesh=mesh, in_specs=in_specs, out_specs=out_specs, check_vma=False)
```

```python
import functools
import math

import jax
import jax.numpy as jnp
from jax import lax
from jax.experimental import pallas as pl
from jax.experimental.pallas import tpu as pltpu
from jax.sharding import PartitionSpec as P


LOG2E = math.log2(math.e)
VM = pl.BlockSpec(memory_space=pltpu.VMEM)
FAR = pl.BlockSpec(memory_space=pltpu.HBM)


def kernel_call(body, outs, scratch=(), in_specs=None, out_specs=None, aliases=None, flops=1 << 22):
    return pl.pallas_call(
        body,
        out_shape=[o if hasattr(o, "dtype") else jax.ShapeDtypeStruct(o, jnp.float32) for o in outs],
        out_specs=out_specs or [VM] * len(outs),
        scratch_shapes=list(scratch),
        input_output_aliases=aliases or {},
        compiler_params=pltpu.CompilerParams(vmem_limit_bytes=24 << 20),
        cost_estimate=pl.CostEstimate(flops=flops, bytes_accessed=1 << 21, transcendentals=0),
        **({} if in_specs is None else {"in_specs": in_specs}),
    )


def split3(x):
    high = x.astype(jnp.bfloat16)
    rest = x - high.astype(jnp.float32)
    middle = rest.astype(jnp.bfloat16)
    low = (rest - middle.astype(jnp.float32)).astype(jnp.bfloat16)
    return high, middle, low


def column_of(row):
    n = row.shape[1]
    r = lax.broadcasted_iota(jnp.int32, (n, n), 0)
    c = lax.broadcasted_iota(jnp.int32, (n, n), 1)
    return jnp.sum(jnp.where(r == c, jnp.broadcast_to(row, (n, n)), 0.0), axis=1, keepdims=True)


def around(v):
    width = v.shape[1]
    return pltpu.roll(v, width - 1, 1) + pltpu.roll(v, 1, 1) - 4.0 * v


def pack_kernel(cap, packed, kept, *refs):
    n_in = kept + 3 + packed
    given, rest = refs[:n_in], refs[n_in:]
    outs, scratch, sems = rest[: 1 + packed + kept], rest[1 + packed + kept : -1], rest[-1]
    scratch, spare = scratch[: 3 + packed], scratch[3 + packed :]
    targets = tuple(scratch) + tuple(outs[1 + packed :])
    copies = [pltpu.make_async_copy(g, t, sems.at[i]) for i, (g, t) in enumerate(zip(given, targets))]
    for copy in copies:
        copy.start()
    fields = outs[0]
    if packed:
        factors, blocks = scratch[0], spare[0]
        tiles, rows, _ = blocks.shape
        top = factors.shape[0] - rows
        lane = lax.broadcasted_iota(jnp.int32, (rows, 2 * cap), 1)
        copies[0].wait()
        for pair in range(tiles // 2):
            first = factors[0:rows, pair * 2 * cap : (pair + 1) * 2 * cap]
            second = factors[top : top + rows, pair * 2 * cap : (pair + 1) * 2 * cap]
            blocks[2 * pair] = jnp.where(lane < cap, first, pltpu.roll(second, cap, 1))
            blocks[2 * pair + 1] = jnp.where(lane < cap, pltpu.roll(first, cap, 1), second)
        parts = [pl.ds(p * (tiles // 4), tiles // 4) for p in range(4)]
        sending = [pltpu.make_async_copy(blocks.at[p], outs[1].at[p], sems.at[n_in + i]) for i, p in enumerate(parts)]
        for copy in sending:
            copy.start()
    kelvin, moisture, spread = scratch[packed:]
    for copy in copies[packed : packed + 3]:
        copy.wait()
    levels = kelvin.shape[0]
    for l in range(levels):
        fields[l : l + 1, :] = kelvin[l]
        fields[levels + l : levels + l + 1, :] = moisture[l]
    fields[2 * levels : 2 * levels + 1, :] = spread[...]
    left = fields.shape[0] - 2 * levels - 1
    if left:
        fields[2 * levels + 1 :, :] = jnp.zeros((left, fields.shape[1]), jnp.float32)
    for copy in copies[packed + 3 :]:
        copy.wait()
    if packed:
        for copy in sending:
            copy.wait()


def prepare_kernel(cap, tiles, levels, fields, near, *refs):
    given, (slot, dry, base, part, inverse, marker), rest = refs[:7], refs[7:13], refs[13:]
    targets, sems = rest[:-1], rest[-1]
    _, _, _, owners, arid, angle, lit = targets
    copies = [pltpu.make_async_copy(g, t, sems.at[i]) for i, (g, t) in enumerate(zip(given, targets))]
    for copy in copies:
        copy.start()
    f = fields[...]
    spread = fields[2 * levels : 2 * levels + 1, :]
    first = f + spread * around(f)
    other = near[...]
    v = spread * other
    side = v + spread * (around(v) + other + near[2 * levels : 2 * levels + 1, :] * (f + around(other)))
    part[...] = side
    base[...] = first + spread * around(first) + side
    for copy in copies:
        copy.wait()
    inverse[...] = 1.0 / angle[...]
    marker[...] = angle[...] * lit[...].astype(jnp.float32)
    columns = owners.shape[1]
    gpoints = arid.shape[0]
    owner = owners[...]
    matches = lax.broadcasted_iota(jnp.int32, (tiles, columns), 0) == owner
    member = matches.astype(jnp.float32)
    r = lax.broadcasted_iota(jnp.int32, (columns, columns), 0)
    c = lax.broadcasted_iota(jnp.int32, (columns, columns), 1)
    earlier = (r < c).astype(jnp.float32).astype(jnp.bfloat16)
    counts = jnp.dot(member.astype(jnp.bfloat16), earlier, preferred_element_type=jnp.float32)
    rank = jnp.sum(jnp.where(matches, counts, 0.0), axis=0, keepdims=True)
    slot[...] = owner * cap + rank.astype(jnp.int32)
    for l in range(levels):
        dry[l] = jnp.broadcast_to(arid[:, l : l + 1] * -LOG2E, (gpoints, dry.shape[2]))


def select_kernel(cap, tiles, packed, scale, homed, slot, vapour, black, solar, weights, black_column, solar_column):
    gpoints = weights.shape[0]
    if packed:
        rows = homed.shape[1]
        lane = lax.broadcasted_iota(jnp.int32, (rows, 2 * cap), 1)
        lower, upper = [], []
        for pair in range(tiles // 2):
            first, second = homed[2 * pair], homed[2 * pair + 1]
            lower.append(jnp.where(lane < cap, first, pltpu.roll(second, cap, 1)))
            upper.append(jnp.where(lane < cap, pltpu.roll(first, cap, 1), second))
        lower = jnp.concatenate(lower, axis=1)
        upper = jnp.concatenate(upper, axis=1)[2 * rows - gpoints :]
        table = jnp.concatenate([lower, upper], axis=0)
    else:
        table = homed[...]
    chosen = lax.broadcasted_iota(jnp.int32, (tiles * cap, slot.shape[1]), 0) == slot[...]
    choice = chosen.astype(jnp.float32).astype(jnp.bfloat16)
    picked = 0.0
    for part in split3(table):
        picked = picked + jnp.dot(part, choice, preferred_element_type=jnp.float32)
    weights[...] = picked * (column_of(vapour[...]) * -LOG2E)
    for row, column in ((black, black_column), (solar, solar_column)):
        column[...] = jnp.broadcast_to(column_of(row[...]) * scale, column.shape)


def side_kernel(levels, fields, near, far, base, part, share, total):
    row = slice(2 * levels, 2 * levels + 1)
    add = (fields[row, :] * near[row, :]) * far[...]
    share[...] = part[...] + add
    total[...] = base[...] + add


def spread_rows(levels, base, share, temp, wet):
    f = base[...] + share[...]
    for l in range(levels):
        temp[l] = f[l : l + 1]
        wet[l] = f[levels + l : levels + l + 1]


def tree_sum(terms):
    terms = list(terms)
    while len(terms) > 1:
        terms = [sum(terms[i + 1 : i + 2], terms[i]) for i in range(0, len(terms), 2)]
    return terms[0]


def unrolled(levels, most):
    return max(u for u in range(1, most + 1) if levels % u == 0)


UD, UU = 90, 90


def radiation_kernel(
    levels, gpoints, first, temp, wet, weights, dry, angle, lit, black, solar, part, rest, steps, sums
):
    blocks = gpoints // 8
    parity = lax.rem(lax.axis_index("grp"), 2)
    half = 1 - parity if first else parity
    at = pl.ds(pl.multiple_of(half * 128, 128), 128)
    inverse = jnp.broadcast_to(angle[:, at], (8, 128))
    marker = jnp.broadcast_to(lit[:, at], (8, 128))
    share_of = [black[8 * b : 8 * b + 8] for b in range(blocks)]
    weight = [weights[8 * b : 8 * b + 8, at] for b in range(blocks)]
    beams = tuple(solar[8 * b : 8 * b + 8] * marker for b in range(blocks))
    zero = jnp.zeros((8, 128), jnp.float32)

    def level(l):
        return pl.ds(pl.multiple_of(l * 8, 8), 8)

    def down_level(l, carry):
        down, beam = carry
        warm = jnp.broadcast_to(temp[l, :, at], (8, 128))
        moist = jnp.broadcast_to(wet[l, :, at], (8, 128))
        sums[level(l), :] = tree_sum(beam)
        new_down, new_beam = [], []
        for b in range(blocks):
            tau = dry[l, 8 * b : 8 * b + 8, :] + weight[b] * moist
            kept = jnp.exp2(tau)
            rest[l, 8 * b : 8 * b + 8, :] = kept
            steps[l, 8 * b : 8 * b + 8, :] = down[b]
            new_beam.append(beam[b] * jnp.exp2(tau * inverse))
            new_down.append(warm + kept * (down[b] - warm))
        return tuple(new_down), tuple(new_beam)

    def up_level(i, carry):
        up, below = carry
        l = levels - 1 - i
        warm = jnp.broadcast_to(temp[l, :, at], (8, 128))
        new_up, terms = [], [sums[level(l), :]]
        for b in range(blocks):
            u = warm + rest[l, 8 * b : 8 * b + 8, :] * (up[b] - warm)
            terms.append(share_of[b] * (steps[l, 8 * b : 8 * b + 8, :] - u))
            new_up.append(u)
        flux = tree_sum(terms)
        part[l] = jnp.sum(flux - below, axis=0, keepdims=True)
        return tuple(new_up), flux

    down, beam = lax.fori_loop(
        0, levels, down_level, ((zero,) * blocks, beams), unroll=unrolled(levels, UD)
    )
    floor = jnp.broadcast_to(temp[levels - 1, :, at], (8, 128))
    ground = tree_sum([s * (d - floor) for s, d in zip(share_of, down)] + list(beam))
    lax.fori_loop(0, levels, up_level, ((floor,) * blocks, ground), unroll=unrolled(levels, UU))


def first_half_kernel(
    levels, gpoints, base, share, weights, dry, angle, lit, black, solar, part, temp, wet, *scratch
):
    spread_rows(levels, base, share, temp, wet)
    radiation_kernel(levels, gpoints, True, temp, wet, weights, dry, angle, lit, black, solar, part, *scratch)


def second_half_kernel(
    levels, gpoints, temp, wet, weights, dry, angle, lit, black, solar, part, vapour, rest, steps, sums, sem
):
    copy = pltpu.make_async_copy(wet, vapour, sem)
    copy.start()
    radiation_kernel(
        levels, gpoints, False, temp, wet, weights, dry, angle, lit, black, solar, part, rest, steps, sums
    )
    copy.wait()


def finish_kernel(own_half, piece, temp, *refs):
    heating, temp_next, warm, sems = refs[-4:]
    parity = lax.rem(lax.axis_index("grp"), 2)
    half = parity if own_half else 1 - parity
    at = pl.ds(pl.multiple_of(half * 128, 128), 128)
    first = pltpu.make_async_copy(piece, heating.at[:, :, at], sems.at[0])
    first.start()
    for l in range(temp.shape[0]):
        warm[l] = temp[l, :, at] + piece[l]
    second = pltpu.make_async_copy(warm, temp_next.at[:, :, at], sems.at[1])
    second.start()
    first.wait()
    second.wait()


def on_device(
    n_tile,
    n_grp,
    kelvin,
    moisture,
    spreading_number,
    angle,
    lit,
    owners,
    factors,
    arid,
    vapour_absorption,
    black,
    solar,
):
    levels, rows, width = kelvin.shape
    gpoints, slots = factors.shape
    cap = slots // n_tile
    total_g = gpoints * n_grp
    if rows != 1 or n_grp & (n_grp - 1) or n_grp < 2 or gpoints % 8 or width != 256:
        raise ValueError("unsupported shapes")
    stacked = -(-(2 * levels + 1) // 8) * 8
    packed = 2 * cap == 128 and gpoints % 16 == 8 and n_tile % 2 == 0
    half = (gpoints + 8) // 2
    inputs = [factors] * packed + [kelvin, moisture, spreading_number]
    row = (1, gpoints)
    kept = [vapour_absorption.reshape(row), black.reshape(row), solar.reshape(row)]
    local = [owners.reshape(1, width), arid, angle, lit]
    outs = [jax.ShapeDtypeStruct((stacked, width), jnp.float32)]
    outs += [jax.ShapeDtypeStruct((n_tile, half, 128), jnp.float32)] * packed
    results = kernel_call(
        functools.partial(pack_kernel, cap, packed, 0),
        outs,
        scratch=[pltpu.VMEM(v.shape, v.dtype) for v in inputs]
        + [pltpu.VMEM((n_tile, half, 128), jnp.float32)] * packed
        + [pltpu.SemaphoreType.DMA((len(inputs) + 4 * packed,))],
        in_specs=[FAR] * len(inputs),
        out_specs=[VM] + [FAR] * packed,
    )(*(pltpu.with_memory_space_constraint(v, pltpu.HBM) for v in inputs))
    fields = results[0]
    if packed:
        homed = lax.all_to_all(results[1], "tile", split_axis=0, concat_axis=0, tiled=True)
    else:
        blocks = factors.reshape(gpoints, n_tile, cap)
        homed = lax.all_to_all(blocks, "tile", split_axis=1, concat_axis=1, tiled=True)
        homed = homed.reshape(gpoints, slots)

    def from_side(distance):
        pairs = []
        for t in range(n_tile):
            for g in range(n_grp):
                s = t - distance if g % 2 == 0 else t + distance
                if 0 <= s < n_tile:
                    pairs.append((s * n_grp + g, t * n_grp + g))
        return lax.ppermute(fields, ("tile", "grp"), pairs)

    def swapped(x, bit):
        return lax.ppermute(x, "grp", [(i, i ^ bit) for i in range(n_grp)])

    near = from_side(1)
    far = from_side(2)
    slot, dry, base, side, inverse, marker, *kept_rows = kernel_call(
        functools.partial(prepare_kernel, cap, n_tile, levels),
        [jax.ShapeDtypeStruct((1, width), jnp.int32), (levels, gpoints, 128)]
        + [(stacked, width)] * 2
        + [(1, width)] * 2
        + [row] * len(kept),
        scratch=[pltpu.VMEM(v.shape, v.dtype) for v in local]
        + [pltpu.SemaphoreType.DMA((len(kept) + len(local),))],
        in_specs=[VM] * 2 + [FAR] * (len(kept) + len(local)),
    )(fields, near, *(pltpu.with_memory_space_constraint(v, pltpu.HBM) for v in kept + local))
    weights, black_column, solar_column = kernel_call(
        functools.partial(select_kernel, cap, n_tile, packed, 1.0 / total_g),
        [(gpoints, width), (gpoints, 128), (gpoints, 128)],
    )(homed, slot, *kept_rows)
    share, mine = kernel_call(
        functools.partial(side_kernel, levels), [(stacked, width)] * 2
    )(fields, near, far, base, side)
    other = swapped(share, 1)
    tables = (weights, dry, inverse, marker, black_column, solar_column)
    work = [
        pltpu.VMEM((levels, gpoints, 128), jnp.float32),
        pltpu.VMEM((levels, gpoints, 128), jnp.float32),
        pltpu.VMEM((levels * 8, 128), jnp.float32),
    ]
    given, temp, wet = kernel_call(
        functools.partial(first_half_kernel, levels, gpoints),
        [(levels, 1, 128), (levels, 1, width), (levels, 1, width)],
        scratch=work,
    )(mine, other, *tables)
    taken = swapped(given, 1)
    part, vapour_next = kernel_call(
        functools.partial(second_half_kernel, levels, gpoints),
        [(levels, 1, 128), (levels, 1, width)],
        scratch=work + [pltpu.SemaphoreType.DMA],
        out_specs=[VM, FAR],
    )(temp, wet, *tables)
    part = part + taken
    bit = 2
    while bit < n_grp:
        part = part + swapped(part, bit)
        bit *= 2
    far_half = swapped(part, 1)
    held = [pltpu.VMEM((levels, 1, 128), jnp.float32), pltpu.SemaphoreType.DMA((2,))]
    results = ()
    for own_half, piece in ((True, part), (False, far_half)):
        results = kernel_call(
            functools.partial(finish_kernel, own_half),
            [(levels, 1, width)] * 2,
            scratch=held,
            in_specs=[VM] * 2 + [FAR] * len(results),
            out_specs=[FAR] * 2,
            aliases={2: 0, 3: 1} if results else {},
        )(piece, temp, *results)
    heating, temp_next = results
    return heating, temp_next, vapour_next


def solution(mesh):
    in_specs = (
        P(None, "tile", None),
        P(None, "tile", None),
        P("tile", None),
        P("tile", None),
        P("tile", None),
        P("tile", None),
        P("grp", "tile"),
        P("grp", None),
        P("grp"),
        P("grp"),
        P("grp"),
    )
    out_specs = (P(None, "tile", None), P(None, "tile", None), P(None, "tile", None))

    def body(*args):
        return on_device(mesh.shape["tile"], mesh.shape["grp"], *args)

    return jax.shard_map(body, mesh=mesh, in_specs=in_specs, out_specs=out_specs, check_vma=False)
```

```python
import functools
import math

import jax
import jax.numpy as jnp
from jax import lax
from jax.experimental import pallas as pl
from jax.experimental.pallas import tpu as pltpu
from jax.sharding import PartitionSpec as P


LOG2E = math.log2(math.e)
VM = pl.BlockSpec(memory_space=pltpu.VMEM)
FAR = pl.BlockSpec(memory_space=pltpu.HBM)


def kernel_call(body, outs, scratch=(), in_specs=None, out_specs=None, aliases=None, flops=1 << 22):
    return pl.pallas_call(
        body,
        out_shape=[o if hasattr(o, "dtype") else jax.ShapeDtypeStruct(o, jnp.float32) for o in outs],
        out_specs=out_specs or [VM] * len(outs),
        scratch_shapes=list(scratch),
        input_output_aliases=aliases or {},
        compiler_params=pltpu.CompilerParams(vmem_limit_bytes=24 << 20),
        cost_estimate=pl.CostEstimate(flops=flops, bytes_accessed=1 << 21, transcendentals=0),
        **({} if in_specs is None else {"in_specs": in_specs}),
    )


def split3(x):
    high = x.astype(jnp.bfloat16)
    rest = x - high.astype(jnp.float32)
    middle = rest.astype(jnp.bfloat16)
    low = (rest - middle.astype(jnp.float32)).astype(jnp.bfloat16)
    return high, middle, low


def column_of(row):
    n = row.shape[1]
    r = lax.broadcasted_iota(jnp.int32, (n, n), 0)
    c = lax.broadcasted_iota(jnp.int32, (n, n), 1)
    return jnp.sum(jnp.where(r == c, jnp.broadcast_to(row, (n, n)), 0.0), axis=1, keepdims=True)


def around(v):
    width = v.shape[1]
    return pltpu.roll(v, width - 1, 1) + pltpu.roll(v, 1, 1) - 4.0 * v


def pack_kernel(cap, packed, kept, *refs):
    n_in = kept + 3 + packed
    given, rest = refs[:n_in], refs[n_in:]
    outs, scratch, sems = rest[: 1 + packed + kept], rest[1 + packed + kept : -1], rest[-1]
    scratch, spare = scratch[: 3 + packed], scratch[3 + packed :]
    targets = tuple(scratch) + tuple(outs[1 + packed :])
    copies = [pltpu.make_async_copy(g, t, sems.at[i]) for i, (g, t) in enumerate(zip(given, targets))]
    for copy in copies:
        copy.start()
    fields = outs[0]
    if packed:
        factors, blocks = scratch[0], spare[0]
        tiles, rows, _ = blocks.shape
        top = factors.shape[0] - rows
        lane = lax.broadcasted_iota(jnp.int32, (rows, 2 * cap), 1)
        copies[0].wait()
        for pair in range(tiles // 2):
            first = factors[0:rows, pair * 2 * cap : (pair + 1) * 2 * cap]
            second = factors[top : top + rows, pair * 2 * cap : (pair + 1) * 2 * cap]
            blocks[2 * pair] = jnp.where(lane < cap, first, pltpu.roll(second, cap, 1))
            blocks[2 * pair + 1] = jnp.where(lane < cap, pltpu.roll(first, cap, 1), second)
        sending = pltpu.make_async_copy(blocks, outs[1], sems.at[n_in])
        sending.start()
    kelvin, moisture, spread = scratch[packed:]
    for copy in copies[packed : packed + 3]:
        copy.wait()
    levels = kelvin.shape[0]
    for l in range(levels):
        fields[l : l + 1, :] = kelvin[l]
        fields[levels + l : levels + l + 1, :] = moisture[l]
    fields[2 * levels : 2 * levels + 1, :] = spread[...]
    left = fields.shape[0] - 2 * levels - 1
    if left:
        fields[2 * levels + 1 :, :] = jnp.zeros((left, fields.shape[1]), jnp.float32)
    for copy in copies[packed + 3 :]:
        copy.wait()
    if packed:
        sending.wait()


def prepare_kernel(cap, tiles, levels, fields, near, *refs):
    given, (slot, dry, base, part, inverse, marker), rest = refs[:7], refs[7:13], refs[13:]
    targets, sems = rest[:-1], rest[-1]
    _, _, _, owners, arid, angle, lit = targets
    copies = [pltpu.make_async_copy(g, t, sems.at[i]) for i, (g, t) in enumerate(zip(given, targets))]
    for copy in copies:
        copy.start()
    f = fields[...]
    spread = fields[2 * levels : 2 * levels + 1, :]
    first = f + spread * around(f)
    other = near[...]
    v = spread * other
    side = v + spread * (around(v) + other + near[2 * levels : 2 * levels + 1, :] * (f + around(other)))
    part[...] = side
    base[...] = first + spread * around(first) + side
    for copy in copies:
        copy.wait()
    inverse[...] = 1.0 / angle[...]
    marker[...] = angle[...] * lit[...].astype(jnp.float32)
    columns = owners.shape[1]
    gpoints = arid.shape[0]
    owner = owners[...]
    matches = lax.broadcasted_iota(jnp.int32, (tiles, columns), 0) == owner
    member = matches.astype(jnp.float32)
    r = lax.broadcasted_iota(jnp.int32, (columns, columns), 0)
    c = lax.broadcasted_iota(jnp.int32, (columns, columns), 1)
    earlier = (r < c).astype(jnp.float32).astype(jnp.bfloat16)
    counts = jnp.dot(member.astype(jnp.bfloat16), earlier, preferred_element_type=jnp.float32)
    rank = jnp.sum(jnp.where(matches, counts, 0.0), axis=0, keepdims=True)
    slot[...] = owner * cap + rank.astype(jnp.int32)
    for l in range(levels):
        dry[l] = jnp.broadcast_to(arid[:, l : l + 1] * -LOG2E, (gpoints, dry.shape[2]))


def select_kernel(cap, tiles, packed, scale, homed, slot, vapour, black, solar, weights, black_column, solar_column):
    gpoints = weights.shape[0]
    if packed:
        rows = homed.shape[1]
        lane = lax.broadcasted_iota(jnp.int32, (rows, 2 * cap), 1)
        lower, upper = [], []
        for pair in range(tiles // 2):
            first, second = homed[2 * pair], homed[2 * pair + 1]
            lower.append(jnp.where(lane < cap, first, pltpu.roll(second, cap, 1)))
            upper.append(jnp.where(lane < cap, pltpu.roll(first, cap, 1), second))
        lower = jnp.concatenate(lower, axis=1)
        upper = jnp.concatenate(upper, axis=1)[2 * rows - gpoints :]
        table = jnp.concatenate([lower, upper], axis=0)
    else:
        table = homed[...]
    chosen = lax.broadcasted_iota(jnp.int32, (tiles * cap, slot.shape[1]), 0) == slot[...]
    choice = chosen.astype(jnp.float32).astype(jnp.bfloat16)
    picked = 0.0
    for part in split3(table):
        picked = picked + jnp.dot(part, choice, preferred_element_type=jnp.float32)
    weights[...] = picked * (column_of(vapour[...]) * -LOG2E)
    for row, column in ((black, black_column), (solar, solar_column)):
        column[...] = jnp.broadcast_to(column_of(row[...]) * scale, column.shape)


def side_kernel(levels, fields, near, far, base, part, share, total):
    row = slice(2 * levels, 2 * levels + 1)
    add = (fields[row, :] * near[row, :]) * far[...]
    share[...] = part[...] + add
    total[...] = base[...] + add


def spread_rows(levels, base, share, temp, wet):
    f = base[...] + share[...]
    for l in range(levels):
        temp[l] = f[l : l + 1]
        wet[l] = f[levels + l : levels + l + 1]


def tree_sum(terms):
    terms = list(terms)
    while len(terms) > 1:
        terms = [sum(terms[i + 1 : i + 2], terms[i]) for i in range(0, len(terms), 2)]
    return terms[0]


def unrolled(levels, most):
    return max(u for u in range(1, most + 1) if levels % u == 0)


UD, UU = 30, 90


def radiation_kernel(
    levels, gpoints, first, temp, wet, weights, dry, angle, lit, black, solar, part, rest, steps, sums
):
    blocks = gpoints // 8
    parity = lax.rem(lax.axis_index("grp"), 2)
    half = 1 - parity if first else parity
    at = pl.ds(pl.multiple_of(half * 128, 128), 128)
    inverse = jnp.broadcast_to(angle[:, at], (8, 128))
    marker = jnp.broadcast_to(lit[:, at], (8, 128))
    share_of = [black[8 * b : 8 * b + 8] for b in range(blocks)]
    weight = [weights[8 * b : 8 * b + 8, at] for b in range(blocks)]
    beams = tuple(solar[8 * b : 8 * b + 8] * marker for b in range(blocks))
    zero = jnp.zeros((8, 128), jnp.float32)

    def level(l):
        return pl.ds(pl.multiple_of(l * 8, 8), 8)

    def down_level(l, carry):
        down, beam = carry
        warm = jnp.broadcast_to(temp[l, :, at], (8, 128))
        moist = jnp.broadcast_to(wet[l, :, at], (8, 128))
        sums[level(l), :] = tree_sum(beam)
        new_down, new_beam = [], []
        for b in range(blocks):
            tau = dry[l, 8 * b : 8 * b + 8, :] + weight[b] * moist
            kept = jnp.exp2(tau)
            rest[l, 8 * b : 8 * b + 8, :] = kept
            steps[l, 8 * b : 8 * b + 8, :] = down[b]
            new_beam.append(beam[b] * jnp.exp2(tau * inverse))
            new_down.append(warm + kept * (down[b] - warm))
        return tuple(new_down), tuple(new_beam)

    def up_level(i, carry):
        up, below = carry
        l = levels - 1 - i
        warm = jnp.broadcast_to(temp[l, :, at], (8, 128))
        new_up, terms = [], [sums[level(l), :]]
        for b in range(blocks):
            u = warm + rest[l, 8 * b : 8 * b + 8, :] * (up[b] - warm)
            terms.append(share_of[b] * (steps[l, 8 * b : 8 * b + 8, :] - u))
            new_up.append(u)
        flux = tree_sum(terms)
        part[l] = jnp.sum(flux - below, axis=0, keepdims=True)
        return tuple(new_up), flux

    down, beam = lax.fori_loop(
        0, levels, down_level, ((zero,) * blocks, beams), unroll=unrolled(levels, UD)
    )
    floor = jnp.broadcast_to(temp[levels - 1, :, at], (8, 128))
    ground = tree_sum([s * (d - floor) for s, d in zip(share_of, down)] + list(beam))
    lax.fori_loop(0, levels, up_level, ((floor,) * blocks, ground), unroll=unrolled(levels, UU))


def first_half_kernel(
    levels, gpoints, base, share, weights, dry, angle, lit, black, solar, part, temp, wet, *scratch
):
    spread_rows(levels, base, share, temp, wet)
    radiation_kernel(levels, gpoints, True, temp, wet, weights, dry, angle, lit, black, solar, part, *scratch)


def second_half_kernel(
    levels, gpoints, temp, wet, weights, dry, angle, lit, black, solar, part, vapour, rest, steps, sums, sem
):
    copy = pltpu.make_async_copy(wet, vapour, sem)
    copy.start()
    radiation_kernel(
        levels, gpoints, False, temp, wet, weights, dry, angle, lit, black, solar, part, rest, steps, sums
    )
    copy.wait()


def finish_kernel(own_half, piece, temp, *refs):
    heating, temp_next, warm, sems = refs[-4:]
    parity = lax.rem(lax.axis_index("grp"), 2)
    half = parity if own_half else 1 - parity
    at = pl.ds(pl.multiple_of(half * 128, 128), 128)
    first = pltpu.make_async_copy(piece, heating.at[:, :, at], sems.at[0])
    first.start()
    for l in range(temp.shape[0]):
        warm[l] = temp[l, :, at] + piece[l]
    second = pltpu.make_async_copy(warm, temp_next.at[:, :, at], sems.at[1])
    second.start()
    first.wait()
    second.wait()


def on_device(
    n_tile,
    n_grp,
    kelvin,
    moisture,
    spreading_number,
    angle,
    lit,
    owners,
    factors,
    arid,
    vapour_absorption,
    black,
    solar,
):
    levels, rows, width = kelvin.shape
    gpoints, slots = factors.shape
    cap = slots // n_tile
    total_g = gpoints * n_grp
    if rows != 1 or n_grp & (n_grp - 1) or n_grp < 2 or gpoints % 8 or width != 256:
        raise ValueError("unsupported shapes")
    stacked = -(-(2 * levels + 1) // 8) * 8
    packed = 2 * cap == 128 and gpoints % 16 == 8 and n_tile % 2 == 0
    half = (gpoints + 8) // 2
    inputs = [factors] * packed + [kelvin, moisture, spreading_number]
    row = (1, gpoints)
    kept = [vapour_absorption.reshape(row), black.reshape(row), solar.reshape(row)]
    local = [owners.reshape(1, width), arid, angle, lit]
    outs = [jax.ShapeDtypeStruct((stacked, width), jnp.float32)]
    outs += [jax.ShapeDtypeStruct((n_tile, half, 128), jnp.float32)] * packed
    results = kernel_call(
        functools.partial(pack_kernel, cap, packed, 0),
        outs,
        scratch=[pltpu.VMEM(v.shape, v.dtype) for v in inputs]
        + [pltpu.VMEM((n_tile, half, 128), jnp.float32)] * packed
        + [pltpu.SemaphoreType.DMA((len(inputs) + packed,))],
        in_specs=[FAR] * len(inputs),
        out_specs=[VM] + [FAR] * packed,
    )(*(pltpu.with_memory_space_constraint(v, pltpu.HBM) for v in inputs))
    fields = results[0]
    if packed:
        homed = lax.all_to_all(results[1], "tile", split_axis=0, concat_axis=0, tiled=True)
    else:
        blocks = factors.reshape(gpoints, n_tile, cap)
        homed = lax.all_to_all(blocks, "tile", split_axis=1, concat_axis=1, tiled=True)
        homed = homed.reshape(gpoints, slots)

    def from_side(distance):
        pairs = []
        for t in range(n_tile):
            for g in range(n_grp):
                s = t - distance if g % 2 == 0 else t + distance
                if 0 <= s < n_tile:
                    pairs.append((s * n_grp + g, t * n_grp + g))
        return lax.ppermute(fields, ("tile", "grp"), pairs)

    def swapped(x, bit):
        return lax.ppermute(x, "grp", [(i, i ^ bit) for i in range(n_grp)])

    near = from_side(1)
    far = from_side(2)
    slot, dry, base, side, inverse, marker, *kept_rows = kernel_call(
        functools.partial(prepare_kernel, cap, n_tile, levels),
        [jax.ShapeDtypeStruct((1, width), jnp.int32), (levels, gpoints, 128)]
        + [(stacked, width)] * 2
        + [(1, width)] * 2
        + [row] * len(kept),
        scratch=[pltpu.VMEM(v.shape, v.dtype) for v in local]
        + [pltpu.SemaphoreType.DMA((len(kept) + len(local),))],
        in_specs=[VM] * 2 + [FAR] * (len(kept) + len(local)),
    )(fields, near, *(pltpu.with_memory_space_constraint(v, pltpu.HBM) for v in kept + local))
    weights, black_column, solar_column = kernel_call(
        functools.partial(select_kernel, cap, n_tile, packed, 1.0 / total_g),
        [(gpoints, width), (gpoints, 128), (gpoints, 128)],
    )(homed, slot, *kept_rows)
    share, mine = kernel_call(
        functools.partial(side_kernel, levels), [(stacked, width)] * 2
    )(fields, near, far, base, side)
    other = swapped(share, 1)
    tables = (weights, dry, inverse, marker, black_column, solar_column)
    work = [
        pltpu.VMEM((levels, gpoints, 128), jnp.float32),
        pltpu.VMEM((levels, gpoints, 128), jnp.float32),
        pltpu.VMEM((levels * 8, 128), jnp.float32),
    ]
    given, temp, wet = kernel_call(
        functools.partial(first_half_kernel, levels, gpoints),
        [(levels, 1, 128), (levels, 1, width), (levels, 1, width)],
        scratch=work,
    )(mine, other, *tables)
    taken = swapped(given, 1)
    part, vapour_next = kernel_call(
        functools.partial(second_half_kernel, levels, gpoints),
        [(levels, 1, 128), (levels, 1, width)],
        scratch=work + [pltpu.SemaphoreType.DMA],
        out_specs=[VM, FAR],
    )(temp, wet, *tables)
    part = part + taken
    bit = 2
    while bit < n_grp:
        part = part + swapped(part, bit)
        bit *= 2
    far_half = swapped(part, 1)
    held = [pltpu.VMEM((levels, 1, 128), jnp.float32), pltpu.SemaphoreType.DMA((2,))]
    results = ()
    for own_half, piece in ((True, part), (False, far_half)):
        results = kernel_call(
            functools.partial(finish_kernel, own_half),
            [(levels, 1, width)] * 2,
            scratch=held,
            in_specs=[VM] * 2 + [FAR] * len(results),
            out_specs=[FAR] * 2,
            aliases={2: 0, 3: 1} if results else {},
        )(piece, temp, *results)
    heating, temp_next = results
    return heating, temp_next, vapour_next


def solution(mesh):
    in_specs = (
        P(None, "tile", None),
        P(None, "tile", None),
        P("tile", None),
        P("tile", None),
        P("tile", None),
        P("tile", None),
        P("grp", "tile"),
        P("grp", None),
        P("grp"),
        P("grp"),
        P("grp"),
    )
    out_specs = (P(None, "tile", None), P(None, "tile", None), P(None, "tile", None))

    def body(*args):
        return on_device(mesh.shape["tile"], mesh.shape["grp"], *args)

    return jax.shard_map(body, mesh=mesh, in_specs=in_specs, out_specs=out_specs, check_vma=False)
```
